128 devices in a mesh: dp: 8 (over z_hi, y), seq: 16 (over x, z_lo, core).
Axes of the slice: x: 4, y: 4, z: 4 (z_hi: 2, z_lo: 2; z = z_hi * 2 + z_lo), core: 2. Of those that a mesh axis runs over, the one named last changes fastest.
Arguments:
- sequence: bfloat16 [8, 8192, 384], P('dp', 'seq'), may hold values from -200 to 200
- conv_weight: bfloat16 [2, 3, 384, 384], replicated, may hold values from -0.1875 to 0.1875
- batch_norm_gains: float32 [3, 384], replicated, may hold values from 0.25 to 1.75
- batch_norm_shifts: float32 [3, 384], replicated, may hold values from -0.5 to 0.5
- head_weight: bfloat16 [384, 5313], replicated, may hold values from -0.3125 to 0.3125
- head_bias: float32 [5313], replicated, may hold values from -1 to 1
- targets: int32 [8, 8192, 5313], P('dp', 'seq'), may hold values from 0 to 31
Outputs:
- grad_input: float32 [8, 8192, 384], P('dp', 'seq')
- grad_conv: float32 [2, 3, 384, 384], replicated
- grad_gain: float32 [3, 384], replicated
- grad_shift: float32 [3, 384], replicated
- grad_head: float32 [384, 5313], P('seq')
- grad_head_bias: float32 [5313], replicated
The draws below stay inside these ranges and needn't reach their ends.
All inputs are finite; a program needn't handle non-finite values.
Results may differ from the reference program's by a relative error of at most 0.0057.
Values may be sent and summed in bfloat16 or wider, within the bound.
A program may use at most 128 MiB of HBM per device.

```python
import math
import jax
import jax.numpy as jnp
import numpy as np
from jax import lax

C = 384
TRACKS = 5313
NBINS = 8192
LOCI = 8
NEAR_DILATION = 2048
FAR_DILATION = 4096


def draw_sequence(key, part):
    key_noise, key_chan = jax.random.split(jax.random.fold_in(key, 17), 2)
    places = jnp.arange(NBINS, dtype=jnp.float32) / NBINS
    loci = jnp.arange(LOCI, dtype=jnp.float32) / max(LOCI - 1, 1)
    ramp = (1.0 + 2.0 * loci)[:, None, None] * (1.0 + 2.0 * places)[None, :, None]
    noise = jax.random.normal(key_noise, (LOCI, NBINS, C), jnp.float32)
    offset = 0.5 * jax.random.normal(key_chan, (C,), jnp.float32)
    values = noise * ramp + offset * ramp
    return jnp.clip(values, -200.0, 200.0).astype(jnp.bfloat16)


def set_ends(result, stream_key, smallest, high):
    longest = result.shape.index(max(result.shape))
    spots = []
    for shift in (0, 1):
        where = [jax.random.randint(jax.random.fold_in(stream_key, axis), (), 0, length) for axis, length in enumerate(result.shape)]
        where[longest] = (where[longest] + shift) % result.shape[longest]
        spots.append(tuple(where))
    return result.at[spots[0]].set(smallest).at[spots[1]].set(high)


def rank_bounds(count, lean):
    weights = [(1 << 20) // math.isqrt(grade ** lean) + 1 for grade in range(1, count + 1)]
    scale = 1 + sum(weights) // (1 << 30)
    return np.cumsum(np.array([max(1, weight // scale) for weight in weights]))


def ranked_ids(key, dims, amount, skew):
    listing = rank_bounds(amount, skew)
    lot = jax.random.randint(jax.random.fold_in(key, 1), dims, 0, int(listing[amount - 1]))
    standing = jnp.searchsorted(jnp.asarray(listing, jnp.int32), lot, side="right")
    return jax.random.permutation(jax.random.fold_in(key, 2), amount)[standing].astype(jnp.int32)


def centred(own_key, extent, width, most, kind=jnp.bfloat16):
    return jnp.clip(width * jax.random.normal(own_key, extent, jnp.float32), -most, most).astype(kind)


def setup_inputs(seed: int = 0) -> dict:
    key_of = jax.random.split(jax.random.key(seed), 8)
    return {
        "sequence": draw_sequence(jax.random.fold_in(key_of[7], 71), 0),
        "conv_weight": centred(key_of[1], (2, 3, C, C), (3 * C) ** -0.5, 0.1875),
        "batch_norm_gains": jnp.clip(1.0 + 0.15 * jax.random.normal(key_of[2], (3, C), jnp.float32), 0.25, 1.75),
        "batch_norm_shifts": jnp.clip(jax.random.uniform(key_of[3], (3, C), jnp.float32, -0.5, 0.5), -0.5, 0.5),
        "head_weight": centred(key_of[4], (C, TRACKS), C ** -0.5, 0.3125),
        "head_bias": jnp.clip(jax.random.uniform(key_of[5], (TRACKS,), jnp.float32, -1.0, 1.0), -1.0, 1.0),
        "targets": set_ends(ranked_ids(key_of[6], (LOCI, NBINS, TRACKS), 32, 2), jax.random.fold_in(key_of[6], 3), 0, 31).astype(jnp.int32),
    }


EPS = 1e-05

def exact_gelu_fn(value):
    return jax.nn.gelu(value, approximate=False)

def project(block, weight):
    flat = block.reshape(-1, block.shape[-1])
    return jnp.dot(flat, weight, preferred_element_type=jnp.float32).reshape(block.shape[:-1] + (weight.shape[-1],))

def contract(left, right):
    return lax.dot_general(left.reshape(-1, left.shape[-1]), right.reshape(-1, right.shape[-1]), (((0,), (0,)), ((), ())), preferred_element_type=jnp.float32)

def taps(block, dist):
    zeros = jnp.zeros_like(block[:, :dist])
    lower_neighbour = jnp.concatenate([zeros, block[:, :-dist]], axis=1)
    upper_neighbour = jnp.concatenate([block[:, dist:], zeros], axis=1)
    return (lower_neighbour, upper_neighbour)

def batch_norm_forward(residual_field, norm_gain_value, norm_shift_value):
    batch_mean = lax.optimization_barrier(jnp.mean(residual_field, axis=(0, 1)))
    centered_input = residual_field - batch_mean
    var = lax.optimization_barrier(jnp.mean(centered_input * centered_input, axis=(0, 1)))
    inverse_deviation = lax.rsqrt(var + EPS)
    normalized_input = centered_input * inverse_deviation
    preactivation = normalized_input * norm_gain_value + norm_shift_value
    return (exact_gelu_fn(preactivation).astype(jnp.bfloat16), preactivation, normalized_input, inverse_deviation)

def gelu_back(preactivation, upstream):
    return jax.vjp(exact_gelu_fn, preactivation)[1](upstream)[0]

def batch_norm_backward(preact_gradient, normalized_input, inverse_deviation, norm_gain_value, element_count):
    first_layer = lax.optimization_barrier(jnp.sum(preact_gradient, axis=(0, 1)))
    second_layer = lax.optimization_barrier(jnp.sum(preact_gradient * normalized_input, axis=(0, 1)))
    field_gradient = norm_gain_value * inverse_deviation * (preact_gradient - first_layer / element_count - normalized_input * second_layer / element_count)
    return (field_gradient, second_layer, first_layer)

def reference(sequence, conv_weight, batch_norm_gains, batch_norm_shifts, head_weight, head_bias, targets):
    element_count = LOCI * NBINS
    dilation_list = (NEAR_DILATION, FAR_DILATION)
    residual_field = sequence.astype(jnp.float32)
    saved_tensors = []
    for layer_number in range(2):
        activation_out, preactivation, normalized_input, inverse_deviation = batch_norm_forward(residual_field, batch_norm_gains[layer_number], batch_norm_shifts[layer_number])
        lower_neighbour, upper_neighbour = taps(activation_out, dilation_list[layer_number])
        update = project(lower_neighbour, conv_weight[layer_number, 0]) + project(activation_out, conv_weight[layer_number, 1]) + project(upper_neighbour, conv_weight[layer_number, 2])
        saved_tensors.append((activation_out, lower_neighbour, upper_neighbour, preactivation, normalized_input, inverse_deviation))
        residual_field = residual_field + update
    hidden_state, final_preactivation, final_normalized, final_inverse_deviation = batch_norm_forward(residual_field, batch_norm_gains[2], batch_norm_shifts[2])
    scale = 1.0 / math.sqrt(LOCI * NBINS)

    def head_step(carry, item):
        rows, counts = item
        logits = jnp.dot(rows, head_weight, preferred_element_type=jnp.float32) + head_bias
        dlogit = ((jnp.exp(logits) - counts.astype(jnp.float32)) * scale).astype(jnp.bfloat16)
        weight_sum = carry[0] + lax.dot_general(rows, dlogit, (((0,), (0,)), ((), ())), preferred_element_type=jnp.float32)
        bias_sum = carry[1] + lax.optimization_barrier(jnp.sum(dlogit.astype(jnp.float32), axis=0))
        dhidden = lax.dot_general(dlogit, head_weight, (((1,), (1,)), ((), ())), preferred_element_type=jnp.float32)
        return ((weight_sum, bias_sum), dhidden)
    start = (jnp.zeros((C, TRACKS), jnp.float32), jnp.zeros((TRACKS,), jnp.float32))
    (grad_head, grad_head_bias), dhidden = lax.scan(head_step, start, (hidden_state, targets))
    preact_gradient = gelu_back(final_preactivation, dhidden)
    field_grad_input, last_gain, last_shift = batch_norm_backward(preact_gradient, final_normalized, final_inverse_deviation, batch_norm_gains[2], element_count)
    gain_list = [None, None, last_gain]
    shift_list = [None, None, last_shift]
    conv_grads = [None, None]
    for layer_number in (1, 0):
        activation_out, lower_neighbour, upper_neighbour, preactivation, normalized_input, inverse_deviation = saved_tensors[layer_number]
        grad_low = field_grad_input.astype(jnp.bfloat16)
        below, above = taps(grad_low, dilation_list[layer_number])
        dact = project(above, conv_weight[layer_number, 0].T) + project(grad_low, conv_weight[layer_number, 1].T) + project(below, conv_weight[layer_number, 2].T)
        conv_grads[layer_number] = jnp.stack([contract(lower_neighbour, grad_low), contract(activation_out, grad_low), contract(upper_neighbour, grad_low)])
        preact_gradient = gelu_back(preactivation, dact)
        field_gradient, gain_list[layer_number], shift_list[layer_number] = batch_norm_backward(preact_gradient, normalized_input, inverse_deviation, batch_norm_gains[layer_number], element_count)
        field_grad_input = field_grad_input + field_gradient
    return (field_grad_input, jnp.stack(conv_grads), jnp.stack(gain_list), jnp.stack(shift_list), grad_head, grad_head_bias)
```

```python
import functools
import math

import jax
import jax.numpy as jnp
from jax import lax
from jax.experimental import pallas as pl
from jax.experimental.pallas import tpu as pltpu
from jax.sharding import PartitionSpec as P

MESH = pl.DeviceIdType.MESH
F32 = jnp.float32
BF16 = jnp.bfloat16
EPS = 1e-05
C = 384
R = 512
Q = 128
TW = 768
CH = 32
PAD = 256
NDEV = 128


def nn(a, b):
    return lax.dot_general(a, b, (((1,), (0,)), ((), ())), preferred_element_type=F32)


def nt(a, b):
    return lax.dot_general(a, b, (((1,), (1,)), ((), ())), preferred_element_type=F32)


def fold(v):
    return v.reshape(v.shape[0] // 8, 8, v.shape[1]).sum(axis=0)


def cdf_of(pre):
    return 0.5 * (1.0 + lax.erf(pre * math.sqrt(0.5)))


def slope_of(pre):
    return cdf_of(pre) + pre * (jnp.exp(-0.5 * pre * pre) * (1.0 / math.sqrt(2.0 * math.pi)))


def kernel(
    seq_ref, gain_ref, shift_ref, hb_ref, cw_hbm, hw_hbm, tg_hbm,
    gin_ref, ggain_ref, gshift_ref, ghead_ref, gbias_ref, gconv_ref,
    cw, hw, tg, xq, x1, x2, act0, act1, actT0, actT1, hs, h, hT, dz, dhacc, dhs, dhq, gp0, gp1, gp2, gpad, g, dpre, asend, arecv,
    b1, b2, load_sem, s1_sem, s2_sem, r1_sem, r2_sem, as_sem, ar_sem,
):
    dp = lax.axis_index("dp")
    sq = lax.axis_index("seq")
    x, zl, core = sq // 4, (sq // 2) % 2, sq % 2
    zh, y = dp // 4, dp % 4
    me1 = x * 2 + core
    me2 = y * 4 + zh * 2 + zl

    loads = [
        pltpu.make_async_copy(cw_hbm, cw, load_sem.at[0]),
        pltpu.make_async_copy(hw_hbm, hw, load_sem.at[1]),
        pltpu.make_async_copy(tg_hbm, tg, load_sem.at[2]),
    ]
    for cp in loads:
        cp.start()

    def peer1(d):
        slot = lax.rem(me1 + d, 8)
        return slot, (dp, (slot // 2) * 4 + zl * 2 + slot % 2)

    def peer2(d):
        slot = lax.rem(me2 + d, 16)
        return slot, (((slot // 2) % 2) * 4 + slot // 4, x * 4 + (slot % 2) * 2 + core)

    def peerx(d):
        slot = lax.rem(x + d, 4)
        return slot, (dp, slot * 4 + zl * 2 + core)

    barrier = pltpu.get_barrier_semaphore()

    @pl.loop(1, 8)
    def _(d):
        pl.semaphore_signal(barrier, inc=1, device_id=peer1(d)[1], device_id_type=MESH)

    @pl.loop(1, 16)
    def _(d):
        pl.semaphore_signal(barrier, inc=1, device_id=peer2(d)[1], device_id_type=MESH)

    def exchange(buf, k, me, count, peer, ssem, rsem, do):
        def cp(d):
            slot, dev = peer(d)
            return slot, dev

        if do == "start":
            @pl.loop(1, count)
            def _(d):
                slot, dev = peer(d)
                pltpu.make_async_remote_copy(
                    src_ref=buf.at[k, me], dst_ref=buf.at[k, me], send_sem=ssem.at[slot], recv_sem=rsem.at[k, me],
                    device_id=dev, device_id_type=MESH,
                ).start()
        else:
            @pl.loop(1, count)
            def _(d):
                slot, dev = peer(d)
                pltpu.make_async_remote_copy(
                    src_ref=buf.at[k, me], dst_ref=buf.at[k, slot], send_sem=ssem.at[slot], recv_sem=rsem.at[k, slot],
                    device_id=dev, device_id_type=MESH,
                ).wait()

    def merge(buf, k, count, each, forward):
        parts = [buf[k, i] for i in range(count)]
        total = functools.reduce(lambda a, b: a + b, parts)
        if not forward:
            return total
        mean = total[0:1] * (1.0 / count)
        dev = functools.reduce(lambda a, b: a + b, [jnp.square(p[0:1] - mean) for p in parts])
        return jnp.concatenate([mean, total[1:2] + each * dev], axis=0)

    def sync(k, value, forward, work1=None, work2=None):
        b1[k, me1] = value
        exchange(b1, k, me1, 8, peer1, s1_sem, r1_sem, "start")
        if work1 is not None:
            work1()
        exchange(b1, k, me1, 8, peer1, s1_sem, r1_sem, "wait")
        b2[k, me2] = merge(b1, k, 8, float(R), forward)
        exchange(b2, k, me2, 16, peer2, s2_sem, r2_sem, "start")
        if work2 is not None:
            work2()
        exchange(b2, k, me2, 16, peer2, s2_sem, r2_sem, "wait")
        return merge(b2, k, 16, float(R * 8), forward)

    def a2a(n, src, dst, do):
        for d in range(1, 4):
            slot, dev = peerx(d)
            mine = pltpu.make_async_remote_copy(
                src_ref=src.at[slot], dst_ref=dst.at[x], send_sem=as_sem.at[n, d], recv_sem=ar_sem.at[n, x],
                device_id=dev, device_id_type=MESH,
            )
            if do == "start":
                mine.start()
            else:
                mine.wait_send()
                pltpu.make_async_remote_copy(
                    src_ref=src.at[slot], dst_ref=dst.at[slot], send_sem=as_sem.at[n, d], recv_sem=ar_sem.at[n, slot],
                    device_id=dev, device_id_type=MESH,
                ).wait_recv()

    def chunks(body, init=None, step=CH):
        def f(i, carry):
            return body(pl.multiple_of(i * step, step), carry)
        return lax.fori_loop(0, R // step, f, init)

    def stats(load):
        zero = jnp.zeros((8, C), F32)
        total = chunks(lambda o, acc: acc + fold(load(o)), zero)
        mean = jnp.sum(total, axis=0, keepdims=True) * (1.0 / R)
        m2 = chunks(lambda o, acc: acc + fold(jnp.square(load(o) - mean)), zero)
        return jnp.concatenate([mean, jnp.sum(m2, axis=0, keepdims=True)], axis=0)

    first = stats(lambda o: seq_ref[pl.ds(o, CH), :].astype(F32))
    pl.semaphore_wait(barrier, 22)

    for d in range(1, 4):
        slot, dev = peerx(d)
        pltpu.make_async_remote_copy(
            src_ref=seq_ref.at[pl.ds(pl.multiple_of(slot * Q, Q), Q)], dst_ref=xq.at[x], send_sem=as_sem.at[0, d],
            recv_sem=ar_sem.at[0, x], device_id=dev, device_id_type=MESH,
        ).start()

    def begin():
        xq[x] = seq_ref[pl.ds(pl.multiple_of(x * Q, Q), Q), :]
        zeros = jnp.zeros((PAD, C), BF16)
        for buf in (act0, act1, gpad):
            buf[0:PAD] = zeros
            buf[PAD + R:] = zeros
        a2a(0, xq, xq, "wait")
        loads[0].wait()

    def load0(o):
        return xq[o // Q, pl.ds(lax.rem(o, Q), CH), :].astype(F32)

    def loader(ref):
        return lambda o: ref[pl.ds(o, CH), :]

    load_x = [load0, loader(x1), loader(x2)]
    acts, actTs, gps = [act0, act1, None], [actT0, actT1], [gp0, gp1, gp2]
    norms = []

    def norm(k, moments):
        inv = lax.rsqrt(moments[1:2] * (1.0 / (R * NDEV)) + EPS)
        norms.append((moments[0:1], inv, gain_ref[k:k + 1, :], shift_ref[k:k + 1, :]))

    def xhat_at(k, o):
        mean, inv, _, _ = norms[k]
        return (load_x[k](o) - mean) * inv

    def pre_at(k, o):
        return xhat_at(k, o) * norms[k][2] + norms[k][3]

    def activate(k, store):
        def body(o, _):
            pre = pre_at(k, o)
            store(o, (pre * cdf_of(pre)).astype(BF16))
        chunks(body)

    def slopes(k):
        def body(o, _):
            gps[k][pl.ds(o, CH), :] = slope_of(pre_at(k, o))
        chunks(body)

    moments = sync(0, first, True, begin)
    norm(0, moments)
    outs = [x1, x2]
    spans = (Q, 2 * Q)
    for l in range(2):
        act, dst, span = acts[l], outs[l], spans[l]

        def keep(o, v, act=act):
            act[pl.ds(PAD + o, CH), :] = v

        activate(l, keep)
        for r in range(0, R, 256):
            acc = nn(act[pl.ds(PAD - span + r, 256), :], cw[l, 0])
            acc += nn(act[pl.ds(PAD + r, 256), :], cw[l, 1])
            acc += nn(act[pl.ds(PAD + span + r, 256), :], cw[l, 2])
            if l == 0:
                old = jnp.concatenate([xq[r // Q], xq[r // Q + 1]], axis=0).astype(F32)
            else:
                old = x1[pl.ds(r, 256), :]
            dst[pl.ds(r, 256), :] = old + acc

        def side(l=l, act=act):
            slopes(l)
            actTs[l][...] = act[pl.ds(PAD, R), :].T

        moments = sync(l + 1, stats(load_x[l + 1]), True, side)
        norm(l + 1, moments)

    def keep_h(o, v):
        hs[o // Q, pl.ds(lax.rem(o, Q), CH), :] = v

    activate(2, keep_h)
    a2a(1, hs, h, "start")
    h[x] = hs[x]
    slopes(2)
    loads[1].wait()
    loads[2].wait()
    a2a(1, hs, h, "wait")
    for k in range(4):
        hT[:, k * Q:(k + 1) * Q] = h[k].T
    scale = 1.0 / math.sqrt(R * NDEV)
    tracks = hw.shape[1]

    def tile(start, width, store_dh):
        cols = pl.ds(start, width)
        w = hw[:, cols]
        bias = hb_ref[:, cols]
        total = jnp.zeros((8, width), F32)
        for k in range(4):
            logits = nn(h[k], w) + bias
            counts = tg[pl.ds(k * Q, Q), cols].astype(F32)
            v = ((jnp.exp(logits) - counts) * scale).astype(BF16)
            dz[k * Q:(k + 1) * Q, 0:width] = v
            total = total + fold(v.astype(F32))
            store_dh(k, nt(v, w))
        gbias_ref[:, cols] = jnp.sum(total, axis=0, keepdims=True)
        ghead_ref[:, cols] = nn(hT[...], dz[:, 0:width]).astype(BF16)

    full = tracks // TW

    def put(k, v):
        dhacc[k] = v

    def add(k, v):
        dhacc[k] += v

    tile(full * TW, tracks - full * TW, put)

    @pl.loop(0, full)
    def _(t):
        tile(pl.multiple_of(t * TW, TW), TW, add)

    for k in range(4):
        dhs[k] = dhacc[k].astype(BF16)
    a2a(2, dhs, dhq, "start")
    dhq[x] = dhs[x]
    a2a(2, dhs, dhq, "wait")

    n = float(R * NDEV)

    def sums(k, load):
        def body(o, acc):
            v = load(o) * gps[k][pl.ds(o, CH), :]
            dpre[pl.ds(o, CH), :] = v
            return acc[0] + fold(v), acc[1] + fold(v * xhat_at(k, o))
        zero = jnp.zeros((8, C), F32)
        a, b = chunks(body, (zero, zero))
        return jnp.concatenate([jnp.sum(a, axis=0, keepdims=True), jnp.sum(b, axis=0, keepdims=True)], axis=0)

    def report(k, s):
        gshift_ref[k:k + 1, :] = s[0:1]
        ggain_ref[k:k + 1, :] = s[1:2]

    def dv_at(k, o, s):
        _, inv, gain, _ = norms[k]
        return gain * inv * (dpre[pl.ds(o, CH), :] - s[0:1] * (1.0 / n) - xhat_at(k, o) * (s[1:2] * (1.0 / n)))

    s = sync(3, sums(2, lambda o: dhq[o // Q, pl.ds(lax.rem(o, Q), CH), :].astype(F32)), False)
    report(2, s)

    for l in (1, 0):
        span = spans[l]

        def spread(o, _, l=l, s=s):
            v = dv_at(l + 1, o, s)
            if l == 0:
                v = v + g[pl.ds(o, CH), :]
            g[pl.ds(o, CH), :] = v
            gpad[pl.ds(PAD + o, CH), :] = v.astype(BF16)

        chunks(spread)
        for r in range(0, R, 256):
            acc = nt(gpad[pl.ds(PAD + span + r, 256), :], cw[l, 0])
            acc += nt(gpad[pl.ds(PAD + r, 256), :], cw[l, 1])
            acc += nt(gpad[pl.ds(PAD - span + r, 256), :], cw[l, 2])
            dpre[pl.ds(r, 256), :] = acc

        value = sums(l, lambda o: dpre[pl.ds(o, CH), :])

        def weights(l=l, span=span):
            for j, shift in enumerate((span, 0, -span)):
                gconv_ref[l, j] = nn(actTs[l][...], gpad[pl.ds(PAD + shift, R), :])

        def early(l=l, weights=weights):
            if l == 0:
                _, inv, gain, _ = norms[0]

                def body(o, _):
                    asend[o // Q, pl.ds(lax.rem(o, Q), CH), :] = g[pl.ds(o, CH), :] + gain * inv * dpre[pl.ds(o, CH), :]
                chunks(body)
                a2a(3, asend, arecv, "start")
                arecv[x] = asend[x]
            weights()

        s = sync(5 - l, value, False, early)
        report(l, s)

    a2a(3, asend, arecv, "wait")
    mean, inv, gain, _ = norms[0]

    def finish(o, _):
        xh = (seq_ref[pl.ds(o, CH), :].astype(F32) - mean) * inv
        part = arecv[o // Q, pl.ds(lax.rem(o, Q), CH), :]
        gin_ref[pl.ds(o, CH), :] = part - gain * inv * (s[0:1] * (1.0 / n) + xh * (s[1:2] * (1.0 / n)))
    chunks(finish)


def on_device(sequence, conv_weight, gains, shifts, head_weight, head_bias, targets):
    tracks = head_weight.shape[1]
    vmem = pl.BlockSpec(memory_space=pltpu.VMEM)
    hbm = pl.BlockSpec(memory_space=pl.ANY)
    sds = jax.ShapeDtypeStruct
    V = pltpu.VMEM
    D = pltpu.SemaphoreType.DMA
    gin, ggain, gshift, ghead, gbias, gconv = pl.pallas_call(
        kernel,
        out_shape=(
            sds((R, C), F32), sds((3, C), F32), sds((3, C), F32), sds((C, tracks), BF16), sds((1, tracks), F32),
            sds((2, 3, C, C), F32),
        ),
        in_specs=[vmem, vmem, vmem, vmem, hbm, hbm, hbm],
        out_specs=(vmem,) * 6,
        scratch_shapes=[
            V((2, 3, C, C), BF16), V((C, tracks), BF16), V((R, tracks), jnp.int32),
            V((4, Q, C), BF16), V((R, C), F32), V((R, C), F32),
            V((R + 2 * PAD, C), BF16), V((R + 2 * PAD, C), BF16), V((C, R), BF16), V((C, R), BF16),
            V((4, Q, C), BF16), V((4, Q, C), BF16), V((C, R), BF16), V((R, TW), BF16), V((4, Q, C), F32),
            V((4, Q, C), BF16), V((4, Q, C), BF16),
            V((R, C), F32), V((R, C), F32), V((R, C), F32), V((R + 2 * PAD, C), BF16), V((R, C), F32), V((R, C), F32),
            V((4, Q, C), F32), V((4, Q, C), F32),
            V((6, 8, 2, C), F32), V((6, 16, 2, C), F32),
            D((3,)), D((8,)), D((16,)), D((6, 8)), D((6, 16)), D((4, 4)), D((4, 4)),
        ],
        compiler_params=pltpu.CompilerParams(
            collective_id=0, has_side_effects=True, vmem_limit_bytes=62 * 1024 * 1024
        ),
        name="whole",
    )(sequence.reshape(R, C), gains, shifts, head_bias.reshape(1, tracks), conv_weight, head_weight,
      targets.reshape(R, tracks))
    rows = lax.psum_scatter(ghead, "seq", scatter_dimension=0, tiled=True).astype(F32)
    grad_head = lax.psum(rows, "dp")
    grad_conv, bias = lax.psum((gconv, gbias), ("dp", "seq"))
    return gin.reshape(1, R, C), grad_conv, ggain, gshift, grad_head, bias.reshape(tracks)


def solution(mesh):
    rep = P()
    return jax.shard_map(
        on_device,
        mesh=mesh,
        in_specs=(P("dp", "seq", None), rep, rep, rep, rep, rep, P("dp", "seq", None)),
        out_specs=(P("dp", "seq", None), rep, rep, rep, P("seq", None), rep),
        check_vma=False,
    )
```

```python
import functools
import math

import jax
import jax.numpy as jnp
from jax import lax
from jax.experimental import pallas as pl
from jax.experimental.pallas import tpu as pltpu
from jax.sharding import PartitionSpec as P

MESH = pl.DeviceIdType.MESH
F32 = jnp.float32
BF16 = jnp.bfloat16
EPS = 1e-05
C = 384
R = 512
Q = 128
TW = 768
CH = 32
PAD = 256
NDEV = 128


def nn(a, b):
    return lax.dot_general(a, b, (((1,), (0,)), ((), ())), preferred_element_type=F32)


def nt(a, b):
    return lax.dot_general(a, b, (((1,), (1,)), ((), ())), preferred_element_type=F32)


def fold(v):
    return v.reshape(v.shape[0] // 8, 8, v.shape[1]).sum(axis=0)


def cdf_of(pre):
    return 0.5 * (1.0 + lax.erf(pre * math.sqrt(0.5)))


def slope_of(pre):
    return cdf_of(pre) + pre * (jnp.exp(-0.5 * pre * pre) * (1.0 / math.sqrt(2.0 * math.pi)))


def kernel(
    seq_ref, gain_ref, shift_ref, hb_ref, cw_hbm, hw_hbm, tg_hbm,
    gin_ref, ggain_ref, gshift_ref, ghead_ref, gbias_ref, gconv_ref,
    cw, wt, wtail, w, tg, ttail, bcol, hbp, xq, x1, x2, act0, act1, actT0, actT1, hs, h, hT, hP, hPb, dz, dhacc, dhs, dhq,
    gp0, gp1, gp2, gpad, g, dpre, asend, arecv, b1, b2, bb1, bb2,
    gsend, grecv, gown, xsend, xrecv, zown, zsend, zrecv, dsend, drecv, fall,
    cfull, csend, crecv, cx, cxr, cy, cyr, cz, ca, cb,
    load_sem, s1_sem, s2_sem, r1_sem, r2_sem, as_sem, ar_sem,
    e1_sem, e2_sem, q1_sem, q2_sem, gcs, gcr, gxs, gxr, gzs, gzr, gds, gdr, gfs, gfr,
    ccs, ccr, cxs, cxrs, cys, cyrs, czs, czrs, cas, cars, cbs, cbrs,
):
    dp = lax.axis_index("dp")
    sq = lax.axis_index("seq")
    x, zl, core = sq // 4, (sq // 2) % 2, sq % 2
    zh, y = dp // 4, dp % 4
    me1 = x * 2 + core
    me2 = y * 4 + zh * 2 + zl

    loads = [
        pltpu.make_async_copy(cw_hbm, cw, load_sem.at[0]),
        pltpu.make_async_copy(hw_hbm, wt, load_sem.at[1]),
    ] + [
        pltpu.make_async_copy(tg_hbm.at[:, 0, j * Q:(j + 1) * Q], tg.at[:, j * Q:(j + 1) * Q], load_sem.at[2 + j])
        for j in range(4)
    ]
    for cp in loads:
        cp.start()

    def peer1(d):
        slot = lax.rem(me1 + d, 8)
        return slot, (dp, (slot // 2) * 4 + zl * 2 + slot % 2)

    def peer2(d):
        slot = lax.rem(me2 + d, 16)
        return slot, (((slot // 2) % 2) * 4 + slot // 4, x * 4 + (slot % 2) * 2 + core)

    def peerx(d):
        slot = lax.rem(x + d, 4)
        return slot, (dp, slot * 4 + zl * 2 + core)

    barrier = pltpu.get_barrier_semaphore()

    @pl.loop(1, 8)
    def _(d):
        pl.semaphore_signal(barrier, inc=1, device_id=peer1(d)[1], device_id_type=MESH)

    @pl.loop(1, 16)
    def _(d):
        pl.semaphore_signal(barrier, inc=1, device_id=peer2(d)[1], device_id_type=MESH)

    def exchange(buf, k, me, count, peer, ssem, rsem, do):
        def cp(d):
            slot, dev = peer(d)
            return slot, dev

        if do == "start":
            @pl.loop(1, count)
            def _(d):
                slot, dev = peer(d)
                pltpu.make_async_remote_copy(
                    src_ref=buf.at[k, me], dst_ref=buf.at[k, me], send_sem=ssem.at[slot], recv_sem=rsem.at[k, me],
                    device_id=dev, device_id_type=MESH,
                ).start()
        else:
            @pl.loop(1, count)
            def _(d):
                slot, dev = peer(d)
                pltpu.make_async_remote_copy(
                    src_ref=buf.at[k, me], dst_ref=buf.at[k, slot], send_sem=ssem.at[slot], recv_sem=rsem.at[k, slot],
                    device_id=dev, device_id_type=MESH,
                ).wait()

    def merge(buf, k, count, each, forward):
        parts = [buf[k, i] for i in range(count)]
        total = functools.reduce(lambda a, b: a + b, parts)
        if not forward:
            return total
        mean = total[0:1] * (1.0 / count)
        dev = functools.reduce(lambda a, b: a + b, [jnp.square(p[0:1] - mean) for p in parts])
        return jnp.concatenate([mean, total[1:2] + each * dev], axis=0)

    def sync(k, value, forward, work1=None, work2=None):
        b1[k, me1] = value
        exchange(b1, k, me1, 8, peer1, s1_sem, r1_sem, "start")
        if work1 is not None:
            work1()
        exchange(b1, k, me1, 8, peer1, s1_sem, r1_sem, "wait")
        b2[k, me2] = merge(b1, k, 8, float(R), forward)
        exchange(b2, k, me2, 16, peer2, s2_sem, r2_sem, "start")
        if work2 is not None:
            work2()
        exchange(b2, k, me2, 16, peer2, s2_sem, r2_sem, "wait")
        return merge(b2, k, 16, float(R * 8), forward)

    def a2a(n, src, dst, do):
        for d in range(1, 4):
            slot, dev = peerx(d)
            mine = pltpu.make_async_remote_copy(
                src_ref=src.at[slot], dst_ref=dst.at[x], send_sem=as_sem.at[n, d], recv_sem=ar_sem.at[n, x],
                device_id=dev, device_id_type=MESH,
            )
            if do == "start":
                mine.start()
            else:
                mine.wait_send()
                pltpu.make_async_remote_copy(
                    src_ref=src.at[slot], dst_ref=dst.at[slot], send_sem=as_sem.at[n, d], recv_sem=ar_sem.at[n, slot],
                    device_id=dev, device_id_type=MESH,
                ).wait_recv()

    def chunks(body, init=None, step=CH):
        def f(i, carry):
            return body(pl.multiple_of(i * step, step), carry)
        return lax.fori_loop(0, R // step, f, init)

    def stats(load):
        zero = jnp.zeros((8, C), F32)
        total = chunks(lambda o, acc: acc + fold(load(o)), zero)
        mean = jnp.sum(total, axis=0, keepdims=True) * (1.0 / R)
        m2 = chunks(lambda o, acc: acc + fold(jnp.square(load(o) - mean)), zero)
        return jnp.concatenate([mean, jnp.sum(m2, axis=0, keepdims=True)], axis=0)

    first = stats(lambda o: seq_ref[pl.ds(o, CH), :].astype(F32))
    pl.semaphore_wait(barrier, 22)

    for d in range(1, 4):
        slot, dev = peerx(d)
        pltpu.make_async_remote_copy(
            src_ref=seq_ref.at[pl.ds(pl.multiple_of(slot * Q, Q), Q)], dst_ref=xq.at[x], send_sem=as_sem.at[0, d],
            recv_sem=ar_sem.at[0, x], device_id=dev, device_id_type=MESH,
        ).start()

    def begin():
        xq[x] = seq_ref[pl.ds(pl.multiple_of(x * Q, Q), Q), :]
        zeros = jnp.zeros((PAD, C), BF16)
        for buf in (act0, act1, gpad):
            buf[0:PAD] = zeros
            buf[PAD + R:] = zeros
        a2a(0, xq, xq, "wait")
        loads[0].wait()

    def prepare_bias():
        tracks = hb_ref.shape[0]
        hbp[...] = jnp.zeros(hbp.shape, F32)
        last = tracks // Q * Q
        for i in range(tracks // Q):
            hbp[i:i + 1, :] = hb_ref[pl.ds(i * Q, Q)].reshape(1, Q)
        hbp[tracks // Q:tracks // Q + 1, 0:tracks - last] = hb_ref[pl.ds(last, tracks - last)].reshape(1, tracks - last)

        @pl.loop(0, hbp.shape[0] - 6)
        def _(i):
            bcol[pl.ds(pl.multiple_of(i * Q, Q), Q), :] = jnp.broadcast_to(hbp[pl.ds(i, 1), :], (Q, Q)).T

    def prepare_weights():
        loads[1].wait()
        tracks = wt.shape[0]
        edge = tracks // 256 * 256
        wtail[...] = jnp.zeros(wtail.shape, BF16)
        wtail[0:tracks - edge] = wt[edge:tracks]

        @pl.loop(0, tracks // 256)
        def _(i):
            o = pl.multiple_of(i * 256, 256)
            w[:, pl.ds(o, 256)] = wt[pl.ds(o, 256), :].T
        w[:, edge:edge + 256] = wtail[...].T

    def prepare_counts():
        for cp in loads[2:]:
            cp.wait()
        tracks = tg.shape[0]
        edge = tracks // 256 * 256
        ttail[...] = jnp.zeros(ttail.shape, jnp.int32)
        ttail[0:tracks - edge] = tg[edge:tracks]

    def load0(o):
        return xq[o // Q, pl.ds(lax.rem(o, Q), CH), :].astype(F32)

    def loader(ref):
        return lambda o: ref[pl.ds(o, CH), :]

    load_x = [load0, loader(x1), loader(x2)]
    acts, actTs, gps = [act0, act1, None], [actT0, actT1], [gp0, gp1, gp2]
    norms = []

    def norm(k, moments):
        inv = lax.rsqrt(moments[1:2] * (1.0 / (R * NDEV)) + EPS)
        norms.append((moments[0:1], inv, gain_ref[k:k + 1, :], shift_ref[k:k + 1, :]))

    def xhat_at(k, o):
        mean, inv, _, _ = norms[k]
        return (load_x[k](o) - mean) * inv

    def pre_at(k, o):
        return xhat_at(k, o) * norms[k][2] + norms[k][3]

    def activate(k, store):
        def body(o, _):
            pre = pre_at(k, o)
            store(o, (pre * cdf_of(pre)).astype(BF16))
        chunks(body)

    def slopes(k):
        def body(o, _):
            gps[k][pl.ds(o, CH), :] = slope_of(pre_at(k, o))
        chunks(body)

    moments = sync(0, first, True, begin, prepare_bias)
    norm(0, moments)
    outs = [x1, x2]
    spans = (Q, 2 * Q)
    for l in range(2):
        act, dst, span = acts[l], outs[l], spans[l]

        def keep(o, v, act=act):
            act[pl.ds(PAD + o, CH), :] = v

        activate(l, keep)
        for r in range(0, R, 256):
            acc = nn(act[pl.ds(PAD - span + r, 256), :], cw[l, 0])
            acc += nn(act[pl.ds(PAD + r, 256), :], cw[l, 1])
            acc += nn(act[pl.ds(PAD + span + r, 256), :], cw[l, 2])
            if l == 0:
                old = jnp.concatenate([xq[r // Q], xq[r // Q + 1]], axis=0).astype(F32)
            else:
                old = x1[pl.ds(r, 256), :]
            dst[pl.ds(r, 256), :] = old + acc

        def side(l=l, act=act):
            slopes(l)
            actTs[l][...] = act[pl.ds(PAD, R), :].T

        moments = sync(l + 1, stats(load_x[l + 1]), True, side, (prepare_weights, prepare_counts)[l])
        norm(l + 1, moments)

    tracks = wt.shape[0]
    full = tracks // TW
    rest = tracks - full * TW
    tiles = full + 1
    half = C // 2
    other = (dp, sq + 1 - 2 * core)

    def rcopy(src, dst, ssem, rsem, dev):
        return pltpu.make_async_remote_copy(
            src_ref=src, dst_ref=dst, send_sem=ssem, recv_sem=rsem, device_id=dev, device_id_type=MESH
        )

    def keep_h(o, v):
        hs[o // Q, pl.ds(lax.rem(o, Q), CH), :] = v

    activate(2, keep_h)
    a2a(1, hs, h, "start")
    h[x] = hs[x]
    slopes(2)
    a2a(1, hs, h, "wait")
    for k in range(4):
        part = h[k].T
        hT[:, k * Q:(k + 1) * Q] = part
        wide = part.astype(F32)
        for s in range(16):
            sx, sz, sc = s // 4, (s // 2) % 2, s % 2
            to = jnp.where(core == sc, half, 0) + sx * 48 + sz * 24
            hP[pl.ds(pl.multiple_of(to, 8), 24), k * Q:(k + 1) * Q] = wide[24 * s:24 * s + 24]
    hPb[0:C] = hP[...].astype(BF16)
    ones_row = lax.broadcasted_iota(jnp.int32, (16, R), 0) == 0
    hPb[C:C + 16] = jnp.where(ones_row, 1.0, 0.0).astype(BF16)
    scale = 1.0 / math.sqrt(R * NDEV)

    def piece(rows, counts, bias, at, live):
        v = nn(rows, hT[...])
        for j in range(4):
            z = v[:, j * Q:(j + 1) * Q] + bias
            e = (jnp.exp(z) - counts[:, j * Q:(j + 1) * Q].astype(F32)) * scale
            if live is not None:
                e = jnp.where(lax.broadcasted_iota(jnp.int32, e.shape, 0) < live, e, 0.0)
            dz[at:at + 256, j * Q:(j + 1) * Q] = e.astype(BF16)

    def tile(t, start, tail, first):
        for i in range(3):
            o = start + i * 256 if tail else pl.multiple_of(start + i * 256, 256)
            if tail and i == 2:
                piece(wtail[...], ttail[...], bcol[pl.ds(o, 256), :], i * 256, rest - 512)
            else:
                piece(wt[pl.ds(o, 256), :], tg[pl.ds(o, 256), :], bcol[pl.ds(o, 256), :], i * 256, None)
        part = nt(hPb[...], dz[...])
        gsend[t] = part[0:half].astype(BF16)
        gown[1 if tail else t % 2] = part[half:C]
        bb1[0, me1, pl.ds(t, 1), :] = part[C:C + 1]
        add = nn(w[:, pl.ds(start if tail else pl.multiple_of(start, TW), TW)], dz[...])
        dhacc[...] = add if first else dhacc[...] + add
        rcopy(gsend.at[t], grecv.at[t], gcs.at[t], gcr.at[t], other).start()

    def chip(t):
        rcopy(gsend.at[t], grecv.at[t], gcs.at[t], gcr.at[t], other).wait()
        slot = jnp.where(t == full, 1, t % 2)
        for k in range(4):
            xsend[t, k] = (gown[slot, k * 48:(k + 1) * 48] + grecv[t, k * 48:(k + 1) * 48].astype(F32)).astype(BF16)

    def xstart(t):
        for d in range(1, 4):
            slot, dev = peerx(d)
            rcopy(xsend.at[t, slot], xrecv.at[t, x], gxs.at[t, slot], gxr.at[t, x], dev).start()

    zdev = (dp, x * 4 + (1 - zl) * 2 + core)

    def zstart(t):
        total = xsend[t, x].astype(F32)
        for d in range(1, 4):
            slot, dev = peerx(d)
            rcopy(xsend.at[t, slot], xrecv.at[t, slot], gxs.at[t, slot], gxr.at[t, slot], dev).wait()
            total = total + xrecv[t, slot].astype(F32)
        low, high = total[0:24], total[24:48]
        mine = zl == 0
        zown[t] = jnp.where(mine, low, high)
        zsend[t] = jnp.where(mine, high, low).astype(BF16)
        rcopy(zsend.at[t], zrecv.at[t], gzs.at[t], gzr.at[t], zdev).start()

    def dstart(t):
        rcopy(zsend.at[t], zrecv.at[t], gzs.at[t], gzr.at[t], zdev).wait()
        total = (zown[t] + zrecv[t].astype(F32)).astype(BF16)
        dsend[t] = total

        @pl.when(dp != t)
        def _():
            rcopy(dsend.at[t], drecv.at[dp], gds.at[t], gdr.at[dp], (t, sq)).start()

    def finish_head():
        @pl.loop(0, tiles)
        def _(t):
            @pl.when(dp != t)
            def _():
                rcopy(dsend.at[t], drecv.at[dp], gds.at[t], gdr.at[dp], (t, sq)).wait_send()

        @pl.when(dp < tiles)
        def _():
            total = dsend[dp].astype(F32)
            for d in range(1, 8):
                slot = lax.rem(dp + d, 8)
                rcopy(dsend.at[dp], drecv.at[slot], gds.at[dp], gdr.at[slot], (slot, sq)).wait_recv()
                total = total + drecv[slot].astype(F32)
            fall[dp] = total
            for d in range(1, 8):
                slot = lax.rem(dp + d, 8)
                rcopy(fall.at[dp], fall.at[dp], gfs.at[slot], gfr.at[dp], (slot, sq)).start()

    def collect_head():
        @pl.when(dp < tiles)
        def _():
            for d in range(1, 8):
                slot = lax.rem(dp + d, 8)
                rcopy(fall.at[dp], fall.at[dp], gfs.at[slot], gfr.at[dp], (slot, sq)).wait_send()

        for t in range(tiles):
            @pl.when(dp != t)
            def _():
                rcopy(fall.at[t], fall.at[t], gfs.at[0], gfr.at[t], (t, sq)).wait_recv()
        for t in range(full):
            ghead_ref[:, t * TW:(t + 1) * TW] = fall[t]
        ghead_ref[:, full * TW:tracks] = fall[full][:, 0:rest]

    def bias_start():
        exchange(bb1, 0, me1, 8, peer1, e1_sem, q1_sem, "start")

    def bias_middle():
        exchange(bb1, 0, me1, 8, peer1, e1_sem, q1_sem, "wait")
        bb2[0, me2] = functools.reduce(lambda a, b: a + b, [bb1[0, i] for i in range(8)])
        exchange(bb2, 0, me2, 16, peer2, e2_sem, q2_sem, "start")

    def bias_end():
        exchange(bb2, 0, me2, 16, peer2, e2_sem, q2_sem, "wait")
        gbias_ref[...] = functools.reduce(lambda a, b: a + b, [bb2[0, i] for i in range(16)])

    bb1[0, me1] = jnp.zeros((8, TW), F32)
    tile(full, full * TW, True, True)

    @pl.loop(0, full)
    def _(t):
        tile(t, t * TW, False, False)
        before = jnp.where(t == 0, full, t - 1)
        chip(before)

        @pl.when(t < 3)
        def _():
            xstart(before)

    for k in range(4):
        dhs[k] = dhacc[:, k * Q:(k + 1) * Q].T.astype(BF16)
    a2a(2, dhs, dhq, "start")
    dhq[x] = dhs[x]
    chip(full - 1)
    a2a(2, dhs, dhq, "wait")

    HR = 3 * C // 2

    def conv_start(l, span, actT):
        for j, shift in enumerate((span, 0, -span)):
            cfull[j * C:(j + 1) * C] = nn(actT[...], gpad[pl.ds(PAD + shift, R), :])
        csend[l] = cfull[pl.ds(pl.multiple_of((1 - core) * HR, 64), HR), :].astype(BF16)
        rcopy(csend.at[l], crecv.at[l], ccs.at[l], ccr.at[l], other).start()

    def conv_x(l):
        rcopy(csend.at[l], crecv.at[l], ccs.at[l], ccr.at[l], other).wait()
        for k in range(4):
            mine = cfull[pl.ds(pl.multiple_of(core * HR + k * 144, 16), 144), :]
            cx[l, k] = (mine + crecv[l, k * 144:(k + 1) * 144].astype(F32)).astype(BF16)
        for d in range(1, 4):
            slot, dev = peerx(d)
            rcopy(cx.at[l, slot], cxr.at[l, x], cxs.at[l, slot], cxrs.at[l, x], dev).start()

    def conv_dev(i):
        return (((i // 2) % 2) * 4 + i // 4, x * 4 + (i % 2) * 2 + core)

    def conv_rs(l):
        total = cx[l, x].astype(F32)
        for d in range(1, 4):
            slot, dev = peerx(d)
            rcopy(cx.at[l, slot], cxr.at[l, slot], cxs.at[l, slot], cxrs.at[l, slot], dev).wait()
            total = total + cxr[l, slot].astype(F32)
        for j in range(9):
            cy[l, j] = total[j * 16:(j + 1) * 16].astype(BF16)

            @pl.when(me2 != j)
            def _(j=j):
                rcopy(cy.at[l, j], cyr.at[l, me2], cys.at[l, j], cyrs.at[l, me2], conv_dev(j)).start()

    def conv_ag(l):
        for j in range(9):
            @pl.when(me2 != j)
            def _(j=j):
                rcopy(cy.at[l, j], cyr.at[l, me2], cys.at[l, j], cyrs.at[l, me2], conv_dev(j)).wait_send()

        @pl.when(me2 < 9)
        def _():
            def body(d, total):
                slot, dev = peer2(d)
                rcopy(cyr.at[l, slot], cyr.at[l, slot], cys.at[l, 0], cyrs.at[l, slot], dev).wait_recv()
                return total + cyr[l, slot].astype(F32)
            total = lax.fori_loop(1, 16, body, cy[l, me2].astype(F32))
            cz[l, me2] = total.astype(BF16)

            @pl.loop(1, 16)
            def _(d):
                slot, dev = peer2(d)
                rcopy(cz.at[l, me2], cz.at[l, me2], czs.at[l, slot], czrs.at[l, me2], dev).start()

    def conv_xag(l):
        @pl.when(me2 < 9)
        def _():
            @pl.loop(1, 16)
            def _(d):
                slot, dev = peer2(d)
                rcopy(cz.at[l, me2], cz.at[l, me2], czs.at[l, slot], czrs.at[l, me2], dev).wait_send()

        for j in range(9):
            @pl.when(me2 != j)
            def _(j=j):
                rcopy(cz.at[l, j], cz.at[l, j], czs.at[l, 0], czrs.at[l, j], conv_dev(j)).wait_recv()
        for d in range(1, 4):
            slot, dev = peerx(d)
            rcopy(cz.at[l], ca.at[l, x], cas.at[l, slot], cars.at[l, x], dev).start()
        ca[l, x] = cz[l]

    def conv_cag(l):
        for d in range(1, 4):
            slot, dev = peerx(d)
            rcopy(cz.at[l], ca.at[l, slot], cas.at[l, slot], cars.at[l, slot], dev).wait()
        rcopy(ca.at[l], cb.at[l], cbs.at[l], cbrs.at[l], other).start()
        gconv_ref[l, core] = ca[l]

    def conv_end(l):
        rcopy(ca.at[l], cb.at[l], cbs.at[l], cbrs.at[l], other).wait()
        gconv_ref[l, 1 - core] = cb[l]

    n = float(R * NDEV)

    def sums(k, load):
        def body(o, acc):
            v = load(o) * gps[k][pl.ds(o, CH), :]
            dpre[pl.ds(o, CH), :] = v
            return acc[0] + fold(v), acc[1] + fold(v * xhat_at(k, o))
        zero = jnp.zeros((8, C), F32)
        a, b = chunks(body, (zero, zero))
        return jnp.concatenate([jnp.sum(a, axis=0, keepdims=True), jnp.sum(b, axis=0, keepdims=True)], axis=0)

    def report(k, s):
        gshift_ref[k:k + 1, :] = s[0:1]
        ggain_ref[k:k + 1, :] = s[1:2]

    def dv_at(k, o, s):
        _, inv, gain, _ = norms[k]
        return gain * inv * (dpre[pl.ds(o, CH), :] - s[0:1] * (1.0 / n) - xhat_at(k, o) * (s[1:2] * (1.0 / n)))

    def fill31():
        xstart(2)
        xstart(3)
        bias_start()

    def fill32():
        pl.loop(0, 3)(lambda i: zstart(jnp.where(i == 0, full, i - 1)))

    s = sync(3, sums(2, lambda o: dhq[o // Q, pl.ds(lax.rem(o, Q), CH), :].astype(F32)), False, fill31, fill32)
    report(2, s)

    for l in (1, 0):
        span = spans[l]

        def spread(o, _, l=l, s=s):
            v = dv_at(l + 1, o, s)
            if l == 0:
                v = v + g[pl.ds(o, CH), :]
            g[pl.ds(o, CH), :] = v
            gpad[pl.ds(PAD + o, CH), :] = v.astype(BF16)

        chunks(spread)
        for r in range(0, R, 256):
            acc = nt(gpad[pl.ds(PAD + span + r, 256), :], cw[l, 0])
            acc += nt(gpad[pl.ds(PAD + r, 256), :], cw[l, 1])
            acc += nt(gpad[pl.ds(PAD - span + r, 256), :], cw[l, 2])
            dpre[pl.ds(r, 256), :] = acc

        value = sums(l, lambda o: dpre[pl.ds(o, CH), :])

        def early(l=l, span=span):
            if l == 0:
                _, inv, gain, _ = norms[0]

                def body(o, _):
                    asend[o // Q, pl.ds(lax.rem(o, Q), CH), :] = g[pl.ds(o, CH), :] + gain * inv * dpre[pl.ds(o, CH), :]
                chunks(body)
                a2a(3, asend, arecv, "start")
                arecv[x] = asend[x]
                conv_rs(1)
                conv_start(0, span, actTs[0])
            else:
                conv_start(1, span, actTs[1])
                xstart(4)
                xstart(5)

        def late(l=l):
            if l == 1:
                pl.loop(2, 4)(zstart)
                pl.loop(0, 3)(lambda i: dstart(jnp.where(i == 0, full, i - 1)))
                bias_middle()
                conv_x(1)
            else:
                conv_x(0)
                pl.loop(4, full)(zstart)
                pl.loop(2, 4)(dstart)
                conv_ag(1)

        s = sync(5 - l, value, False, early, late)
        report(l, s)

    a2a(3, asend, arecv, "wait")
    mean, inv, gain, _ = norms[0]

    def finish(o, _):
        xh = (seq_ref[pl.ds(o, CH), :].astype(F32) - mean) * inv
        part = arecv[o // Q, pl.ds(lax.rem(o, Q), CH), :]
        gin_ref[pl.ds(o, CH), :] = part - gain * inv * (s[0:1] * (1.0 / n) + xh * (s[1:2] * (1.0 / n)))
    chunks(finish)
    pl.loop(4, full)(dstart)
    finish_head()
    bias_end()
    conv_rs(0)
    conv_xag(1)
    conv_ag(0)
    conv_xag(0)
    conv_cag(1)
    conv_cag(0)
    collect_head()
    conv_end(1)
    conv_end(0)


def on_device(sequence, conv_weight, gains, shifts, head_weight, head_bias, targets):
    tracks = head_weight.shape[1]
    vmem = pl.BlockSpec(memory_space=pltpu.VMEM)
    hbm = pl.BlockSpec(memory_space=pl.ANY)
    sds = jax.ShapeDtypeStruct
    V = pltpu.VMEM
    D = pltpu.SemaphoreType.DMA
    T7 = tracks // TW + 1
    W7 = T7 * TW
    HR = 3 * C // 2
    gin, ggain, gshift, ghead, gbias, gconv = pl.pallas_call(
        kernel,
        out_shape=(
            sds((R, C), F32), sds((3, C), F32), sds((3, C), F32), sds((C // 16, tracks), F32), sds((8, TW), F32),
            sds((2, 2, 4, 9, 16, C), BF16),
        ),
        in_specs=[vmem, vmem, vmem, vmem, hbm, hbm, hbm],
        out_specs=(vmem,) * 6,
        scratch_shapes=[
            V((2, 3, C, C), BF16), V((tracks, C), BF16), V((256, C), BF16), V((C, W7), BF16),
            V((tracks, R), jnp.int32), V((256, R), jnp.int32), V((W7, Q), F32), V((48, Q), F32),
            V((4, Q, C), BF16), V((R, C), F32), V((R, C), F32),
            V((R + 2 * PAD, C), BF16), V((R + 2 * PAD, C), BF16), V((C, R), BF16), V((C, R), BF16),
            V((4, Q, C), BF16), V((4, Q, C), BF16), V((C, R), BF16), V((C, R), F32), V((C + 16, R), BF16), V((TW, R), BF16),
            V((C, R), F32), V((4, Q, C), BF16), V((4, Q, C), BF16),
            V((R, C), F32), V((R, C), F32), V((R, C), F32), V((R + 2 * PAD, C), BF16), V((R, C), F32), V((R, C), F32),
            V((4, Q, C), F32), V((4, Q, C), F32),
            V((6, 8, 2, C), F32), V((6, 16, 2, C), F32), V((1, 8, 8, TW), F32), V((1, 16, 8, TW), F32),
            V((T7, 192, TW), BF16), V((T7, 192, TW), BF16), V((2, 192, TW), F32),
            V((T7, 4, 48, TW), BF16), V((T7, 4, 48, TW), BF16), V((T7, 24, TW), F32), V((T7, 24, TW), BF16),
            V((T7, 24, TW), BF16), V((8, 24, TW), BF16), V((8, 24, TW), BF16), V((T7, 24, TW), F32),
            V((3 * C, C), F32), V((2, HR, C), BF16), V((2, HR, C), BF16), V((2, 4, 144, C), BF16), V((2, 4, 144, C), BF16),
            V((2, 9, 16, C), BF16), V((2, 16, 16, C), BF16), V((2, 9, 16, C), BF16),
            V((2, 4, 9, 16, C), BF16), V((2, 4, 9, 16, C), BF16),
            D((6,)), D((8,)), D((16,)), D((6, 8)), D((6, 16)), D((4, 4)), D((4, 4)),
            D((8,)), D((16,)), D((1, 8)), D((1, 16)), D((T7,)), D((T7,)), D((T7, 4)), D((T7, 4)), D((T7,)), D((T7,)),
            D((T7,)), D((8,)), D((8,)), D((T7,)),
            D((2,)), D((2,)), D((2, 4)), D((2, 4)), D((2, 9)), D((2, 16)), D((2, 16)), D((2, 9)), D((2, 4)), D((2, 4)),
            D((2,)), D((2,)),
        ],
        compiler_params=pltpu.CompilerParams(
            collective_id=0, has_side_effects=True, vmem_limit_bytes=62 * 1024 * 1024
        ),
        name="whole",
    )(sequence.reshape(R, C), gains, shifts, head_bias, conv_weight, head_weight.T, jnp.transpose(targets, (2, 0, 1)))
    grad_conv = gconv.reshape(2, 3, C, C).astype(F32)
    return gin.reshape(1, R, C), grad_conv, ggain, gshift, ghead, gbias.reshape(-1)[:tracks]


def solution(mesh):
    rep = P()
    return jax.shard_map(
        on_device,
        mesh=mesh,
        in_specs=(P("dp", "seq", None), rep, rep, rep, rep, rep, P("dp", "seq", None)),
        out_specs=(P("dp", "seq", None), rep, rep, rep, P("seq", None), rep),
        check_vma=False,
    )
```

```python
import functools
import math

import jax
import jax.numpy as jnp
from jax import lax
from jax.experimental import pallas as pl
from jax.experimental.pallas import tpu as pltpu
from jax.sharding import PartitionSpec as P

MESH = pl.DeviceIdType.MESH
F32 = jnp.float32
BF16 = jnp.bfloat16
EPS = 1e-05
C = 384
R = 512
Q = 128
TW = 768
CH = 32
PAD = 256
NDEV = 128


def nn(a, b):
    return lax.dot_general(a, b, (((1,), (0,)), ((), ())), preferred_element_type=F32)


def nt(a, b):
    return lax.dot_general(a, b, (((1,), (1,)), ((), ())), preferred_element_type=F32)


def fold(v):
    return v.reshape(v.shape[0] // 8, 8, v.shape[1]).sum(axis=0)


def cdf_of(pre):
    return 0.5 * (1.0 + lax.erf(pre * math.sqrt(0.5)))


def slope_of(pre):
    return cdf_of(pre) + pre * (jnp.exp(-0.5 * pre * pre) * (1.0 / math.sqrt(2.0 * math.pi)))


def kernel(
    seq_ref, gain_ref, shift_ref, hb_ref, cw_hbm, hw_hbm, tg_hbm,
    gin_ref, ggain_ref, gshift_ref, ghead_ref, gbias_ref, gconv_ref,
    cw, wt, wtail, w, tg, ttail, bcol, hbp, xq, x1, x2, x2o, act0, act1, actT0, actT1, hT, hPb, dz, dhacc, dps, dpq,
    gp0, gp1, gpad, g, dpre, arecv, b1, b2, bb1, bb2,
    gsend, grecv, gown, xsend, xrecv, ysend, yrecv, fall, vrecv, vsend, vx,
    cfull, csend, crecv, cx, cxr, cy, cyr, cz, ca, cb,
    load_sem, s1_sem, s2_sem, r1_sem, r2_sem, as_sem, ar_sem,
    e1_sem, e2_sem, q1_sem, q2_sem, gcs, gcr, gxs, gxr, gys, gyr, gfs, gfr, hvs, hvr, hxs, hxr,
    ccs, ccr, cxs, cxrs, cys, cyrs, czs, czrs, cas, cars, cbs, cbrs,
):
    h = asend = dps
    dp = lax.axis_index("dp")
    sq = lax.axis_index("seq")
    x, zl, core = sq // 4, (sq // 2) % 2, sq % 2
    zh, y = dp // 4, dp % 4
    me1 = x * 2 + core
    me2 = y * 4 + zh * 2 + zl
    me3 = x * 4 + zh * 2 + zl

    loads = [
        pltpu.make_async_copy(cw_hbm, cw, load_sem.at[0]),
        pltpu.make_async_copy(hw_hbm, wt, load_sem.at[1]),
    ] + [
        pltpu.make_async_copy(tg_hbm.at[:, 0, j * Q:(j + 1) * Q], tg.at[:, j * Q:(j + 1) * Q], load_sem.at[2 + j])
        for j in range(4)
    ]
    for cp in loads:
        cp.start()

    def peer1(d):
        slot = lax.rem(me1 + d, 8)
        return slot, (dp, (slot // 2) * 4 + zl * 2 + slot % 2)

    def peer2(d):
        slot = lax.rem(me2 + d, 16)
        return slot, (((slot // 2) % 2) * 4 + slot // 4, x * 4 + (slot % 2) * 2 + core)

    def peerx(d):
        slot = lax.rem(x + d, 4)
        return slot, (dp, slot * 4 + zl * 2 + core)

    def peery(d):
        slot = lax.rem(y + d, 4)
        return slot, (zh * 4 + slot, sq)

    def dev2(i):
        return ((i // 2) % 2) * 4 + i // 4, x * 4 + (i % 2) * 2 + core

    def dev3(i):
        return ((i // 2) % 2) * 4 + y, (i // 4) * 4 + (i % 2) * 2 + core

    def peer3(d):
        slot = lax.rem(me3 + d, 16)
        return slot, dev3(slot)

    barrier = pltpu.get_barrier_semaphore()

    @pl.loop(0, 9)
    def _(i):
        slot = lax.rem(x + 1 + i // 3, 4) * 4 + lax.rem(zh * 2 + zl + 1 + i % 3, 4)
        pl.semaphore_signal(barrier, inc=1, device_id=dev3(slot), device_id_type=MESH)

    @pl.loop(1, 8)
    def _(d):
        pl.semaphore_signal(barrier, inc=1, device_id=peer1(d)[1], device_id_type=MESH)

    @pl.loop(1, 16)
    def _(d):
        pl.semaphore_signal(barrier, inc=1, device_id=peer2(d)[1], device_id_type=MESH)

    def exchange(buf, k, me, count, peer, ssem, rsem, do):
        def cp(d):
            slot, dev = peer(d)
            return slot, dev

        if do == "start":
            @pl.loop(1, count)
            def _(d):
                slot, dev = peer(d)
                pltpu.make_async_remote_copy(
                    src_ref=buf.at[k, me], dst_ref=buf.at[k, me], send_sem=ssem.at[slot], recv_sem=rsem.at[k, me],
                    device_id=dev, device_id_type=MESH,
                ).start()
        else:
            @pl.loop(1, count)
            def _(d):
                slot, dev = peer(d)
                pltpu.make_async_remote_copy(
                    src_ref=buf.at[k, me], dst_ref=buf.at[k, slot], send_sem=ssem.at[slot], recv_sem=rsem.at[k, slot],
                    device_id=dev, device_id_type=MESH,
                ).wait()

    def merge(buf, k, count, each, forward):
        parts = [buf[k, i] for i in range(count)]
        total = functools.reduce(lambda a, b: a + b, parts)
        if not forward:
            return total
        mean = total[0:1] * (1.0 / count)
        dev = functools.reduce(lambda a, b: a + b, [jnp.square(p[0:1] - mean) for p in parts])
        return jnp.concatenate([mean, total[1:2] + each * dev], axis=0)

    def sync(k, value, forward, work1=None, work2=None):
        b1[k, me1] = value
        exchange(b1, k, me1, 8, peer1, s1_sem, r1_sem, "start")
        if work1 is not None:
            work1()
        exchange(b1, k, me1, 8, peer1, s1_sem, r1_sem, "wait")
        b2[k, me2] = merge(b1, k, 8, float(R), forward)
        exchange(b2, k, me2, 16, peer2, s2_sem, r2_sem, "start")
        if work2 is not None:
            work2()
        exchange(b2, k, me2, 16, peer2, s2_sem, r2_sem, "wait")
        return merge(b2, k, 16, float(R * 8), forward)

    def a2a(n, src, dst, do):
        for d in range(1, 4):
            slot, dev = peerx(d)
            mine = pltpu.make_async_remote_copy(
                src_ref=src.at[slot], dst_ref=dst.at[x], send_sem=as_sem.at[n, d], recv_sem=ar_sem.at[n, x],
                device_id=dev, device_id_type=MESH,
            )
            if do == "start":
                mine.start()
            else:
                mine.wait_send()
                pltpu.make_async_remote_copy(
                    src_ref=src.at[slot], dst_ref=dst.at[slot], send_sem=as_sem.at[n, d], recv_sem=ar_sem.at[n, slot],
                    device_id=dev, device_id_type=MESH,
                ).wait_recv()

    def chunks(body, init=None, step=CH):
        def f(i, carry):
            return body(pl.multiple_of(i * step, step), carry)
        return lax.fori_loop(0, R // step, f, init)

    def stats(load):
        zero = jnp.zeros((8, C), F32)
        total = chunks(lambda o, acc: acc + fold(load(o)), zero)
        mean = jnp.sum(total, axis=0, keepdims=True) * (1.0 / R)
        m2 = chunks(lambda o, acc: acc + fold(jnp.square(load(o) - mean)), zero)
        return jnp.concatenate([mean, jnp.sum(m2, axis=0, keepdims=True)], axis=0)

    first = stats(lambda o: seq_ref[pl.ds(o, CH), :].astype(F32))
    tracks = hb_ref.shape[0]

    def prepare_bias():
        hbp[...] = jnp.zeros(hbp.shape, F32)
        last = tracks // Q * Q
        for i in range(tracks // Q):
            hbp[i:i + 1, :] = hb_ref[pl.ds(i * Q, Q)].reshape(1, Q)
        hbp[tracks // Q:tracks // Q + 1, 0:tracks - last] = hb_ref[pl.ds(last, tracks - last)].reshape(1, tracks - last)

        @pl.loop(0, hbp.shape[0] - 6)
        def _(i):
            bcol[pl.ds(pl.multiple_of(i * Q, Q), Q), :] = jnp.broadcast_to(hbp[pl.ds(i, 1), :], (Q, Q)).T

    zeros = jnp.zeros((PAD, C), BF16)
    for buf in (act0, act1, gpad):
        buf[0:PAD] = zeros
        buf[PAD + R:] = zeros
    pl.semaphore_wait(barrier, 31)

    def begin():
        for d in range(1, 4):
            slot, dev = peerx(d)
            pltpu.make_async_remote_copy(
                src_ref=seq_ref.at[pl.ds(pl.multiple_of(slot * Q, Q), Q)], dst_ref=xq.at[x], send_sem=as_sem.at[0, d],
                recv_sem=ar_sem.at[0, x], device_id=dev, device_id_type=MESH,
            ).start()
        xq[x] = seq_ref[pl.ds(pl.multiple_of(x * Q, Q), Q), :]

    def prepare_weights():
        loads[1].wait()
        tracks = wt.shape[0]
        edge = tracks // 256 * 256
        wtail[...] = jnp.zeros(wtail.shape, BF16)
        wtail[0:tracks - edge] = wt[edge:tracks]

        @pl.loop(0, tracks // 256)
        def _(i):
            o = pl.multiple_of(i * 256, 256)
            w[:, pl.ds(o, 256)] = wt[pl.ds(o, 256), :].T
        w[:, edge:edge + 256] = wtail[...].T

    def prepare_counts():
        for cp in loads[2:]:
            cp.wait()
        tracks = tg.shape[0]
        edge = tracks // 256 * 256
        ttail[...] = jnp.zeros(ttail.shape, jnp.int32)
        ttail[0:tracks - edge] = tg[edge:tracks]

    def blocked(ref):
        return lambda o: ref[o // Q, pl.ds(lax.rem(o, Q), CH), :].astype(F32)

    def loader(ref):
        return lambda o: ref[pl.ds(o, CH), :]

    load_x = [blocked(xq), loader(x1), blocked(x2)]
    acts, actTs, gps = [act0, act1, None], [actT0, actT1], [gp0, gp1]
    norms = []

    def norm(k, moments):
        inv = lax.rsqrt(moments[1:2] * (1.0 / (R * NDEV)) + EPS)
        norms.append((moments[0:1], inv, gain_ref[k:k + 1, :], shift_ref[k:k + 1, :]))

    def xhat_at(k, o, load=None):
        mean, inv, _, _ = norms[k]
        return ((load or load_x[k])(o) - mean) * inv

    def pre_at(k, o):
        load = blocked(x2o) if k == 2 else None
        return xhat_at(k, o, load) * norms[k][2] + norms[k][3]

    def activate(k, store):
        def body(o, _):
            pre = pre_at(k, o)
            store(o, (pre * cdf_of(pre)).astype(BF16))
        chunks(body)

    def slopes(k):
        def body(o, _):
            gps[k][pl.ds(o, CH), :] = slope_of(pre_at(k, o))
        chunks(body)

    moments = sync(0, first, True, begin, prepare_weights)
    norm(0, moments)
    a2a(0, xq, xq, "wait")
    loads[0].wait()
    spans = (Q, 2 * Q)
    for l in range(2):
        act, span = acts[l], spans[l]

        def keep(o, v, act=act):
            act[pl.ds(PAD + o, CH), :] = v

        activate(l, keep)
        for r in range(0, R, 256):
            acc = nn(act[pl.ds(PAD - span + r, 256), :], cw[l, 0])
            acc += nn(act[pl.ds(PAD + r, 256), :], cw[l, 1])
            acc += nn(act[pl.ds(PAD + span + r, 256), :], cw[l, 2])
            if l == 0:
                old = jnp.concatenate([xq[r // Q], xq[r // Q + 1]], axis=0).astype(F32)
            else:
                old = x1[pl.ds(r, 256), :]
            new = old + acc
            if l == 0:
                x1[pl.ds(r, 256), :] = new
            else:
                x2[r // Q] = new[0:Q]
                x2[r // Q + 1] = new[Q:2 * Q]

        def side(l=l, act=act):
            if l == 1:
                a2a(1, x2, x2o, "start")
                x2o[x] = x2[x]
            slopes(l)
            actTs[l][...] = act[pl.ds(PAD, R), :].T

        moments = sync(l + 1, stats(load_x[l + 1]), True, side, (prepare_bias, prepare_counts)[l])
        norm(l + 1, moments)

    full = tracks // TW
    rest = tracks - full * TW
    tiles = full + 1
    half = C // 2
    other = (dp, sq + 1 - 2 * core)

    def rcopy(src, dst, ssem, rsem, dev):
        return pltpu.make_async_remote_copy(
            src_ref=src, dst_ref=dst, send_sem=ssem, recv_sem=rsem, device_id=dev, device_id_type=MESH
        )

    def keep_h(o, v):
        h[o // Q, pl.ds(lax.rem(o, Q), CH), :] = v

    a2a(1, x2, x2o, "wait")
    activate(2, keep_h)
    for k in range(4):
        part = h[k].T
        hT[:, k * Q:(k + 1) * Q] = part
        wide = part.astype(F32)
        for s in range(16):
            sx, sz, sc = s // 4, (s // 2) % 2, s % 2
            to = jnp.where(core == sc, half, 0) + sx * 48 + sz * 24
            dhacc[pl.ds(pl.multiple_of(to, 8), 24), k * Q:(k + 1) * Q] = wide[24 * s:24 * s + 24]
    hPb[0:C] = dhacc[...].astype(BF16)
    ones_row = lax.broadcasted_iota(jnp.int32, (16, R), 0) == 0
    hPb[C:C + 16] = jnp.where(ones_row, 1.0, 0.0).astype(BF16)
    scale = 1.0 / math.sqrt(R * NDEV)

    def piece(rows, counts, bias, at, live):
        v = nn(rows, hT[...])
        for j in range(4):
            z = v[:, j * Q:(j + 1) * Q] + bias
            e = (jnp.exp(z) - counts[:, j * Q:(j + 1) * Q].astype(F32)) * scale
            if live is not None:
                e = jnp.where(lax.broadcasted_iota(jnp.int32, e.shape, 0) < live, e, 0.0)
            dz[at:at + 256, j * Q:(j + 1) * Q] = e.astype(BF16)

    def tile(t, start, tail, turn):
        for i in range(3):
            o = start + i * 256 if tail else pl.multiple_of(start + i * 256, 256)
            if tail and i == 2:
                piece(wtail[...], ttail[...], bcol[pl.ds(o, 256), :], i * 256, rest - 512)
            else:
                piece(wt[pl.ds(o, 256), :], tg[pl.ds(o, 256), :], bcol[pl.ds(o, 256), :], i * 256, None)
        part = nt(hPb[...], dz[...])
        gsend[t] = part[0:half].astype(BF16)
        gown[turn] = part[half:C]
        bb1[0, me1, pl.ds(t, 1), :] = part[C:C + 1]
        add = nn(w[:, pl.ds(start if tail else pl.multiple_of(start, TW), TW)], dz[...])
        dhacc[...] += add
        rcopy(gsend.at[t], grecv.at[t], gcs.at[t], gcr.at[t], other).start()

    def chip(t, slot):
        rcopy(gsend.at[t], grecv.at[t], gcs.at[t], gcr.at[t], other).wait()
        for k in range(4):
            xsend[t, k] = (gown[slot, k * 48:(k + 1) * 48] + grecv[t, k * 48:(k + 1) * 48].astype(F32)).astype(BF16)

    def xstart(t):
        for d in range(1, 4):
            slot, dev = peerx(d)
            rcopy(xsend.at[t, slot], xrecv.at[t, x], gxs.at[t, slot], gxr.at[t, x], dev).start()

    def owner(t, i):
        return t, x * 4 + i * 2 + core

    def yz(t, i):
        return rcopy(ysend.at[t, i], yrecv.at[me2], gys.at[t, i], gyr.at[me2], owner(t, i))

    def spread_rows(t, total):
        for i in range(2):
            ysend[t, i] = total[i * 24:i * 24 + 24].astype(BF16)

            @pl.when(jnp.logical_or(dp != t, zl != i))
            def _(i=i):
                yz(t, i).start()

    def ystart(t):
        total = xsend[t, x].astype(F32)
        for d in range(1, 4):
            slot, dev = peerx(d)
            rcopy(xsend.at[t, slot], xrecv.at[t, slot], gxs.at[t, slot], gxr.at[t, slot], dev).wait()
            total = total + xrecv[t, slot].astype(F32)
        spread_rows(t, total)

    def vstart(t):
        @pl.when(y != t)
        def _():
            rcopy(xsend.at[t], vrecv.at[y], hvs.at[t], hvr.at[y], (zh * 4 + t, sq)).start()

    def vmid():
        for d in range(1, 4):
            slot, dev = peery(d)
            rcopy(vrecv.at[slot], vrecv.at[slot], hvs.at[slot], hvr.at[slot], dev).wait_recv()
        for k in range(4):
            total = xsend[y, k].astype(F32)
            for d in range(1, 4):
                total = total + vrecv[lax.rem(y + d, 4), k].astype(F32)
            vsend[k] = total.astype(BF16)
        for d in range(1, 4):
            slot, dev = peerx(d)
            rcopy(vsend.at[slot], vx.at[x], hxs.at[slot], hxr.at[x], dev).start()

    def vend():
        total = vsend[x].astype(F32)
        for d in range(1, 4):
            slot, dev = peerx(d)
            rcopy(vsend.at[slot], vx.at[slot], hxs.at[slot], hxr.at[slot], dev).wait()
            total = total + vx[slot].astype(F32)
        spread_rows(y, total)
        for d in range(1, 4):
            slot, dev = peery(d)
            rcopy(xsend.at[slot], vrecv.at[slot], hvs.at[slot], hvr.at[slot], dev).wait_send()

    def finish_head():
        @pl.when(dp < tiles)
        def _():
            near = dp < 4

            def body(d, total):
                slot = jnp.where(near, y * 4 + lax.rem(me2 + d, 4), lax.rem(me2 + d, 16))
                rcopy(yrecv.at[slot], yrecv.at[slot], gys.at[0, 0], gyr.at[slot], dev2(slot)).wait_recv()
                return total + yrecv[slot].astype(F32)
            total = lax.fori_loop(1, jnp.where(near, 4, 16), body, ysend[dp, zl].astype(F32))
            fall[dp] = total.astype(BF16)

            @pl.loop(1, 8)
            def _(d):
                slot = lax.rem(dp + d, 8)
                rcopy(fall.at[dp], fall.at[dp], gfs.at[slot], gfr.at[dp], (slot, sq)).start()

    def collect_head():
        @pl.loop(0, tiles)
        def _(t):
          @pl.when(jnp.logical_or(t >= 4, t == y))
          def _():
            for i in range(2):
                @pl.when(jnp.logical_or(dp != t, zl != i))
                def _(i=i):
                    yz(t, i).wait_send()

        @pl.when(dp < tiles)
        def _():
            @pl.loop(1, 8)
            def _(d):
                slot = lax.rem(dp + d, 8)
                rcopy(fall.at[dp], fall.at[dp], gfs.at[slot], gfr.at[dp], (slot, sq)).wait_send()

        for t in range(tiles):
            @pl.when(dp != t)
            def _(t=t):
                rcopy(fall.at[t], fall.at[t], gfs.at[0], gfr.at[t], (t, sq)).wait_recv()
        for t in range(full):
            ghead_ref[:, t * TW:(t + 1) * TW] = fall[t].astype(F32)
        ghead_ref[:, full * TW:tracks] = fall[full].astype(F32)[:, 0:rest]

    def bias_start():
        exchange(bb1, 0, me1, 8, peer1, e1_sem, q1_sem, "start")

    def bias_middle():
        exchange(bb1, 0, me1, 8, peer1, e1_sem, q1_sem, "wait")
        bb2[0, me2] = functools.reduce(lambda a, b: a + b, [bb1[0, i] for i in range(8)])
        exchange(bb2, 0, me2, 16, peer2, e2_sem, q2_sem, "start")

    def bias_end():
        exchange(bb2, 0, me2, 16, peer2, e2_sem, q2_sem, "wait")
        total = functools.reduce(lambda a, b: a + b, [bb2[0, i] for i in range(16)])
        for t in range(tiles):
            n = min(TW, tracks - t * TW)
            gbias_ref[pl.ds(t * TW, n)] = total[t, 0:n]

    bb1[0, me1] = jnp.zeros((8, TW), F32)
    dhacc[...] = jnp.zeros(dhacc.shape, F32)

    def near(i):
        return lax.rem(y + 1 + i, 4)

    @pl.loop(0, 3)
    def _(i):
        tile(near(i), near(i) * TW, False, i % 2)

        @pl.when(i > 0)
        def _():
            chip(near(i - 1), (i + 1) % 2)
            vstart(near(i - 1))

    tile(full, full * TW, True, 1)
    chip(near(2), 0)
    vstart(near(2))

    @pl.loop(0, 3)
    def _(i):
        t = jnp.where(i == 0, 4, jnp.where(i == 1, y, 5))
        tile(t, t * TW, False, i % 2)
        chip(jnp.where(i == 0, full, jnp.where(i == 1, 4, y)), (i + 1) % 2)

        @pl.when(i == 0)
        def _():
            xstart(full)

    chip(5, 0)

    class Job:
        def __init__(self, number, layer, taps, at, ring, me, peer, dev):
            self.q, self.layer, self.taps, self.at, self.ring = number, layer, taps, at, ring
            self.me, self.peer, self.dev, self.owners = me, peer, dev, 3 * len(taps)

    jobs = (
        Job(0, 1, (0, 1, 2), y, peery, me3, peer3, dev3),
        Job(1, 0, (0, 2), x, peerx, me2, peer2, dev2),
        Job(2, 0, (1,), y, peery, me3, peer3, dev3),
    )

    def conv_start(l, span, actT, taps):
        for j in taps:
            cfull[j] = nn(actT[...], gpad[pl.ds(PAD + (1 - j) * span, R), :])
            csend[l, j] = cfull[j, pl.ds(pl.multiple_of((1 - core) * half, 64), half), :].astype(BF16)
            rcopy(csend.at[l, j], crecv.at[l, j], ccs.at[l, j], ccr.at[l, j], other).start()

    def conv_x(job):
        l, q = job.layer, job.q
        for i, j in enumerate(job.taps):
            rcopy(csend.at[l, j], crecv.at[l, j], ccs.at[l, j], ccr.at[l, j], other).wait()
            for k in range(4):
                mine = cfull[j, pl.ds(pl.multiple_of(core * half + k * 48, 16), 48), :]
                cx[q, i, k] = (mine + crecv[l, j, k * 48:(k + 1) * 48].astype(F32)).astype(BF16)
            for d in range(1, 4):
                slot, dev = job.ring(d)
                rcopy(cx.at[q, i, slot], cxr.at[q, i, job.at], cxs.at[q, i, slot], cxrs.at[q, i, job.at], dev).start()

    def block(job, i):
        q, me = job.q, job.me
        return rcopy(cy.at[q, i], cyr.at[q, me], cys.at[q, i], cyrs.at[q, me], job.dev(i))

    def conv_rs(job):
        q = job.q
        for j in range(len(job.taps)):
            total = cx[q, j, job.at].astype(F32)
            for d in range(1, 4):
                slot, dev = job.ring(d)
                rcopy(cx.at[q, j, slot], cxr.at[q, j, slot], cxs.at[q, j, slot], cxrs.at[q, j, slot], dev).wait()
                total = total + cxr[q, j, slot].astype(F32)
            for b in range(3):
                i = 3 * j + b
                cy[q, i] = total[b * 16:(b + 1) * 16].astype(BF16)

                @pl.when(job.me != i)
                def _(i=i):
                    block(job, i).start()

    def piece_of(job):
        return cz.at[job.q, job.me // 3, job.me % 3]

    def conv_ag(job):
        q = job.q

        @pl.when(job.me < job.owners)
        def _():
            def body(d, total):
                slot, dev = job.peer(d)
                rcopy(cyr.at[q, slot], cyr.at[q, slot], cys.at[q, 0], cyrs.at[q, slot], dev).wait_recv()
                return total + cyr[q, slot].astype(F32)
            total = lax.fori_loop(1, 16, body, cy[q, job.me].astype(F32))
            cz[q, job.me // 3, job.me % 3] = total.astype(BF16)

            @pl.loop(1, 16)
            def _(d):
                slot, dev = job.peer(d)
                rcopy(piece_of(job), piece_of(job), czs.at[q, slot], czrs.at[q, job.me], dev).start()

    def conv_xag(job):
        q = job.q
        for j in range(len(job.taps)):
            for b in range(3):
                i = 3 * j + b

                @pl.when(job.me != i)
                def _(i=i, j=j, b=b):
                    rcopy(cz.at[q, j, b], cz.at[q, j, b], czs.at[q, 0], czrs.at[q, i], job.dev(i)).wait_recv()
            for d in range(1, 4):
                slot, dev = job.ring(d)
                rcopy(cz.at[q, j], ca.at[q, j, job.at], cas.at[q, j, slot], cars.at[q, j, job.at], dev).start()
            ca[q, j, job.at] = cz[q, j]

    def conv_cag(job):
        q = job.q
        for i, j in enumerate(job.taps):
            for d in range(1, 4):
                slot, dev = job.ring(d)
                rcopy(cz.at[q, i], ca.at[q, i, slot], cas.at[q, i, slot], cars.at[q, i, slot], dev).wait()
            rcopy(ca.at[q, i], cb.at[q, i], cbs.at[q, i], cbrs.at[q, i], other).start()
            gconv_ref[job.layer, j, core] = ca[q, i]

    def conv_end(job):
        q = job.q
        for i, j in enumerate(job.taps):
            rcopy(ca.at[q, i], cb.at[q, i], cbs.at[q, i], cbrs.at[q, i], other).wait()
            gconv_ref[job.layer, j, 1 - core] = cb[q, i]
        for i in range(job.owners):
            @pl.when(job.me != i)
            def _(i=i):
                block(job, i).wait_send()

        @pl.when(job.me < job.owners)
        def _():
            @pl.loop(1, 16)
            def _(d):
                slot, dev = job.peer(d)
                rcopy(piece_of(job), piece_of(job), czs.at[q, slot], czrs.at[q, job.me], dev).wait_send()

    n = float(R * NDEV)

    def sums(k, load):
        def body(o, acc):
            v = load(o) * gps[k][pl.ds(o, CH), :]
            dpre[pl.ds(o, CH), :] = v
            return acc[0] + fold(v), acc[1] + fold(v * xhat_at(k, o))
        zero = jnp.zeros((8, C), F32)
        a, b = chunks(body, (zero, zero))
        return jnp.concatenate([jnp.sum(a, axis=0, keepdims=True), jnp.sum(b, axis=0, keepdims=True)], axis=0)

    def report(k, s):
        gshift_ref[k:k + 1, :] = s[0:1]
        ggain_ref[k:k + 1, :] = s[1:2]

    def dv_at(k, o, s):
        _, inv, gain, _ = norms[k]
        v = blocked(dpq)(o) if k == 2 else dpre[pl.ds(o, CH), :]
        return gain * inv * (v - s[0:1] * (1.0 / n) - xhat_at(k, o) * (s[1:2] * (1.0 / n)))

    def back(o, acc):
        k = o // Q
        v = dpre[pl.ds(o, CH), :] * slope_of(pre_at(2, o))
        dps[k, pl.ds(lax.rem(o, Q), CH), :] = v.astype(BF16)
        return acc[0] + fold(v), acc[1] + fold(v * xhat_at(2, o, blocked(x2o)))

    for k in range(4):
        dpre[k * Q:(k + 1) * Q] = dhacc[:, k * Q:(k + 1) * Q].T
    zero = jnp.zeros((8, C), F32)
    left, right = chunks(back, (zero, zero))
    value = jnp.concatenate([jnp.sum(left, axis=0, keepdims=True), jnp.sum(right, axis=0, keepdims=True)], axis=0)

    def fill31():
        bias_start()
        a2a(2, dps, dpq, "start")
        dpq[x] = dps[x]
        xstart(4)
        xstart(5)

    def fill32():
        bias_middle()
        ystart(full)

    s = sync(3, value, False, fill31, fill32)
    report(2, s)
    a2a(2, dps, dpq, "wait")

    for l in (1, 0):
        span = spans[l]

        def spread(o, _, l=l, s=s):
            v = dv_at(l + 1, o, s)
            if l == 0:
                v = v + g[pl.ds(o, CH), :]
            g[pl.ds(o, CH), :] = v
            gpad[pl.ds(PAD + o, CH), :] = v.astype(BF16)

        chunks(spread)
        if l == 0:
            conv_start(0, span, actTs[0], (0, 1, 2))
        for r in range(0, R, 256):
            acc = nt(gpad[pl.ds(PAD + span + r, 256), :], cw[l, 0])
            acc += nt(gpad[pl.ds(PAD + r, 256), :], cw[l, 1])
            acc += nt(gpad[pl.ds(PAD - span + r, 256), :], cw[l, 2])
            dpre[pl.ds(r, 256), :] = acc

        if l == 0:
            conv_x(jobs[1])
            conv_x(jobs[2])
        value = sums(l, lambda o: dpre[pl.ds(o, CH), :])

        def early(l=l, span=span):
            if l == 0:
                conv_ag(jobs[0])
                _, inv, gain, _ = norms[0]

                def body(o, _):
                    v = g[pl.ds(o, CH), :] + gain * inv * dpre[pl.ds(o, CH), :]
                    asend[o // Q, pl.ds(lax.rem(o, Q), CH), :] = v.astype(BF16)
                chunks(body)
                a2a(3, asend, arecv, "start")
                arecv[x] = asend[x]
                conv_rs(jobs[2])
                conv_rs(jobs[1])
            else:
                conv_start(1, span, actTs[1], (0, 1, 2))
                vmid()
                conv_x(jobs[0])

        def late(l=l):
            if l == 1:
                ystart(4)
                ystart(5)
                vend()
                conv_rs(jobs[0])
            else:
                conv_xag(jobs[0])
                conv_ag(jobs[2])
                conv_ag(jobs[1])

        s = sync(5 - l, value, False, early, late)
        report(l, s)

    a2a(3, asend, arecv, "wait")
    mean, inv, gain, _ = norms[0]

    def finish(o, _):
        xh = (seq_ref[pl.ds(o, CH), :].astype(F32) - mean) * inv
        part = blocked(arecv)(o)
        gin_ref[pl.ds(o, CH), :] = part - gain * inv * (s[0:1] * (1.0 / n) + xh * (s[1:2] * (1.0 / n)))
    chunks(finish)
    conv_xag(jobs[2])
    conv_xag(jobs[1])
    finish_head()
    conv_cag(jobs[0])
    bias_end()
    conv_cag(jobs[2])
    conv_cag(jobs[1])
    conv_end(jobs[0])
    collect_head()
    conv_end(jobs[2])
    conv_end(jobs[1])


def emit(gin, ggain, gshift, ghead, gbias, gconv, *rest):
    outs, bufs, wide, isem, osem = rest[:6], rest[6:12], rest[12], rest[13], rest[14]
    ins = [pltpu.make_async_copy(src, dst, isem.at[i]) for i, (src, dst) in
           enumerate(zip((gin, ggain, gshift, ghead, gbias), bufs))]
    taps = [pltpu.make_async_copy(gconv.at[j], bufs[5].at[j], isem.at[5 + j]) for j in range(6)]
    for cp in taps + ins:
        cp.start()
    back = [pltpu.make_async_copy(src, dst, osem.at[i]) for i, (src, dst) in
            enumerate(zip(bufs, (outs[0], outs[2], outs[3], outs[4], outs[5])))]
    send = [pltpu.make_async_copy(wide.at[j], outs[1].at[j], osem.at[5 + j]) for j in range(6)]
    for j in range(6):
        taps[j].wait()
        wide[j] = bufs[5][j].astype(F32)
        send[j].start()
    for a, b in zip(ins, back):
        a.wait()
        b.start()
    for cp in send + back:
        cp.wait()


def on_device(sequence, conv_weight, gains, shifts, head_weight, head_bias, targets):
    tracks = head_weight.shape[1]
    vmem = pl.BlockSpec(memory_space=pltpu.VMEM)
    hbm = pl.BlockSpec(memory_space=pl.ANY)
    sds = jax.ShapeDtypeStruct
    V = pltpu.VMEM
    D = pltpu.SemaphoreType.DMA
    T7 = tracks // TW + 1
    W7 = T7 * TW
    gin, ggain, gshift, ghead, gbias, gconv = pl.pallas_call(
        kernel,
        out_shape=(
            sds((R, C), F32), sds((3, C), F32), sds((3, C), F32), sds((C // 16, tracks), F32), sds((tracks,), F32),
            sds((2, 3, 2, 4, 3, 16, C), BF16),
        ),
        in_specs=[vmem, vmem, vmem, vmem, hbm, hbm, hbm],
        out_specs=(vmem,) * 6,
        scratch_shapes=[
            V((2, 3, C, C), BF16), V((tracks, C), BF16), V((256, C), BF16), V((C, W7), BF16),
            V((tracks, R), jnp.int32), V((256, R), jnp.int32), V((W7, Q), F32), V((48, Q), F32),
            V((4, Q, C), BF16), V((R, C), F32), V((4, Q, C), F32), V((4, Q, C), F32),
            V((R + 2 * PAD, C), BF16), V((R + 2 * PAD, C), BF16), V((C, R), BF16), V((C, R), BF16),
            V((C, R), BF16), V((C + 16, R), BF16), V((TW, R), BF16),
            V((C, R), F32), V((4, Q, C), BF16), V((4, Q, C), BF16),
            V((R, C), F32), V((R, C), F32), V((R + 2 * PAD, C), BF16), V((R, C), F32), V((R, C), F32),
            V((4, Q, C), BF16),
            V((6, 8, 2, C), F32), V((6, 16, 2, C), F32), V((1, 8, 8, TW), F32), V((1, 16, 8, TW), F32),
            V((T7, 192, TW), BF16), V((T7, 192, TW), BF16), V((2, 192, TW), F32),
            V((T7, 4, 48, TW), BF16), V((T7, 4, 48, TW), BF16), V((T7, 2, 24, TW), BF16), V((16, 24, TW), BF16), V((T7, 24, TW), BF16),
            V((4, 4, 48, TW), BF16), V((4, 48, TW), BF16), V((4, 48, TW), BF16),
            V((3, C, C), F32), V((2, 3, C // 2, C), BF16), V((2, 3, C // 2, C), BF16), V((3, 3, 4, 48, C), BF16),
            V((3, 3, 4, 48, C), BF16), V((3, 9, 16, C), BF16), V((3, 16, 16, C), BF16), V((3, 3, 3, 16, C), BF16),
            V((3, 3, 4, 3, 16, C), BF16), V((3, 3, 4, 3, 16, C), BF16),
            D((6,)), D((8,)), D((16,)), D((6, 8)), D((6, 16)), D((4, 4)), D((4, 4)),
            D((8,)), D((16,)), D((1, 8)), D((1, 16)), D((T7,)), D((T7,)), D((T7, 4)), D((T7, 4)), D((T7, 2)), D((16,)),
            D((8,)), D((T7,)), D((4,)), D((4,)), D((4,)), D((4,)),
            D((2, 3)), D((2, 3)), D((3, 3, 4)), D((3, 3, 4)), D((3, 9)), D((3, 16)), D((3, 16)), D((3, 9)), D((3, 3, 4)), D((3, 3, 4)),
            D((3, 3)), D((3, 3)),
        ],
        compiler_params=pltpu.CompilerParams(
            collective_id=0, has_side_effects=True, vmem_limit_bytes=67043328
        ),
        name="whole",
    )(sequence.reshape(R, C), gains, shifts, head_bias, conv_weight, head_weight.T, jnp.transpose(targets, (2, 0, 1)))
    gin, grad_conv, ggain, gshift, ghead, gbias = pl.pallas_call(
        emit,
        out_shape=(
            sds((R, C), F32), sds((6, C, C), F32), sds((3, C), F32), sds((3, C), F32), sds((C // 16, tracks), F32),
            sds((tracks,), F32),
        ),
        in_specs=[hbm] * 6,
        out_specs=(hbm,) * 6,
        scratch_shapes=[
            V((R, C), F32), V((3, C), F32), V((3, C), F32), V((C // 16, tracks), F32), V((tracks,), F32),
            V((6, C, C), BF16), V((6, C, C), F32), D((11,)), D((11,)),
        ],
        name="emit",
    )(gin, ggain, gshift, ghead, gbias, gconv.reshape(6, C, C))
    return gin.reshape(1, R, C), grad_conv.reshape(2, 3, C, C), ggain, gshift, ghead, gbias


def solution(mesh):
    rep = P()
    return jax.shard_map(
        on_device,
        mesh=mesh,
        in_specs=(P("dp", "seq", None), rep, rep, rep, rep, rep, P("dp", "seq", None)),
        out_specs=(P("dp", "seq", None), rep, rep, rep, P("seq", None), rep),
        check_vma=False,
    )
```

```python
import functools
import math

import jax
import jax.numpy as jnp
from jax import lax
from jax.experimental import pallas as pl
from jax.experimental.pallas import tpu as pltpu
from jax.sharding import PartitionSpec as P

MESH = pl.DeviceIdType.MESH
F32 = jnp.float32
BF16 = jnp.bfloat16
EPS = 1e-05
C = 384
R = 512
Q = 128
TW = 768
CH = 32
PAD = 256
NDEV = 128


def nn(a, b):
    return lax.dot_general(a, b, (((1,), (0,)), ((), ())), preferred_element_type=F32)


def nt(a, b):
    return lax.dot_general(a, b, (((1,), (1,)), ((), ())), preferred_element_type=F32)


def fold(v):
    return v.reshape(v.shape[0] // 8, 8, v.shape[1]).sum(axis=0)


def cdf_of(pre):
    return 0.5 * (1.0 + lax.erf(pre * math.sqrt(0.5)))


def slope_of(pre):
    return cdf_of(pre) + pre * (jnp.exp(-0.5 * pre * pre) * (1.0 / math.sqrt(2.0 * math.pi)))


def kernel(
    seq_hbm, gain_hbm, shift_hbm, hb_hbm, cw_hbm, hw_hbm, tg_hbm,
    gin_hbm, ggain_ref, gshift_ref, ghead_hbm, gbias_ref, gconv_hbm,
    seq_ref, gain_ref, shift_ref, hb_ref, ghead_ref,
    cw, wt, wtail, w, tg, ttail, bcol, hbp, xq, x1, x2, x2o, act0, act1, actT0, actT1, hT, hPb, dz, dhacc, dps, dpq,
    gp0, gp1, gpad, g, dpre, arecv, b1, b2, bb1, brow, bin_, ball,
    gsend, grecv, gown, xsend, xrecv, ysend, yrecv, fall, vrecv, vsend, vx,
    cfull, csend, crecv, cx, cxr, cy, cyr, cz, ca, cb,
    load_sem, s1_sem, s2_sem, r1_sem, r2_sem, as_sem, ar_sem,
    e1_sem, e2_sem, q1_sem, q2_sem, brs, brr, gcs, gcr, gxs, gxr, gys, gyr, gfs, gfr, hvs, hvr, hxs, hxr,
    out_sem, oc_sem, ccs, ccr, cxs, cxrs, cys, cyrs, czs, czrs, cas, cars, cbs, cbrs,
):
    h = asend = dps
    dp = lax.axis_index("dp")
    sq = lax.axis_index("seq")
    x, zl, core = sq // 4, (sq // 2) % 2, sq % 2
    zh, y = dp // 4, dp % 4
    me1 = x * 2 + core
    me2 = y * 4 + zh * 2 + zl
    me3 = x * 4 + zh * 2 + zl

    def peer1(d):
        slot = lax.rem(me1 + d, 8)
        return slot, (dp, (slot // 2) * 4 + zl * 2 + slot % 2)

    def peer2(d):
        slot = lax.rem(me2 + d, 16)
        return slot, (((slot // 2) % 2) * 4 + slot // 4, x * 4 + (slot % 2) * 2 + core)

    def peerx(d):
        slot = lax.rem(x + d, 4)
        return slot, (dp, slot * 4 + zl * 2 + core)

    def peery(d):
        slot = lax.rem(y + d, 4)
        return slot, (zh * 4 + slot, sq)

    def dev2(i):
        return ((i // 2) % 2) * 4 + i // 4, x * 4 + (i % 2) * 2 + core

    def dev3(i):
        return ((i // 2) % 2) * 4 + y, (i // 4) * 4 + (i % 2) * 2 + core

    def peer3(d):
        slot = lax.rem(me3 + d, 16)
        return slot, dev3(slot)

    barrier = pltpu.get_barrier_semaphore()

    @pl.loop(0, 9)
    def _(i):
        slot = lax.rem(x + 1 + i // 3, 4) * 4 + lax.rem(zh * 2 + zl + 1 + i % 3, 4)
        pl.semaphore_signal(barrier, inc=1, device_id=dev3(slot), device_id_type=MESH)

    @pl.loop(1, 8)
    def _(d):
        pl.semaphore_signal(barrier, inc=1, device_id=peer1(d)[1], device_id_type=MESH)

    @pl.loop(1, 16)
    def _(d):
        pl.semaphore_signal(barrier, inc=1, device_id=peer2(d)[1], device_id_type=MESH)

    small = [
        pltpu.make_async_copy(src, dst, load_sem.at[6 + i])
        for i, (src, dst) in enumerate(((seq_hbm, seq_ref), (gain_hbm, gain_ref), (shift_hbm, shift_ref), (hb_hbm, hb_ref)))
    ]
    loads = [
        pltpu.make_async_copy(cw_hbm, cw, load_sem.at[0]),
        pltpu.make_async_copy(hw_hbm, wt, load_sem.at[1]),
    ] + [
        pltpu.make_async_copy(tg_hbm.at[:, 0, j * Q:(j + 1) * Q], tg.at[:, j * Q:(j + 1) * Q], load_sem.at[2 + j])
        for j in range(4)
    ]
    for cp in small + loads:
        cp.start()

    def exchange(buf, k, me, count, peer, ssem, rsem, do):
        def cp(d):
            slot, dev = peer(d)
            return slot, dev

        if do == "start":
            @pl.loop(1, count)
            def _(d):
                slot, dev = peer(d)
                pltpu.make_async_remote_copy(
                    src_ref=buf.at[k, me], dst_ref=buf.at[k, me], send_sem=ssem.at[slot], recv_sem=rsem.at[k, me],
                    device_id=dev, device_id_type=MESH,
                ).start()
        else:
            @pl.loop(1, count)
            def _(d):
                slot, dev = peer(d)
                pltpu.make_async_remote_copy(
                    src_ref=buf.at[k, me], dst_ref=buf.at[k, slot], send_sem=ssem.at[slot], recv_sem=rsem.at[k, slot],
                    device_id=dev, device_id_type=MESH,
                ).wait()

    def merge(buf, k, count, each, forward):
        parts = [buf[k, i] for i in range(count)]
        total = functools.reduce(lambda a, b: a + b, parts)
        if not forward:
            return total
        mean = total[0:1] * (1.0 / count)
        dev = functools.reduce(lambda a, b: a + b, [jnp.square(p[0:1] - mean) for p in parts])
        return jnp.concatenate([mean, total[1:2] + each * dev], axis=0)

    def sync(k, value, forward, work1=None, work2=None):
        b1[k, me1] = value
        exchange(b1, k, me1, 8, peer1, s1_sem, r1_sem, "start")
        if work1 is not None:
            work1()
        exchange(b1, k, me1, 8, peer1, s1_sem, r1_sem, "wait")
        b2[k, me2] = merge(b1, k, 8, float(R), forward)
        exchange(b2, k, me2, 16, peer2, s2_sem, r2_sem, "start")
        if work2 is not None:
            work2()
        exchange(b2, k, me2, 16, peer2, s2_sem, r2_sem, "wait")
        return merge(b2, k, 16, float(R * 8), forward)

    def a2a(n, src, dst, do):
        for d in range(1, 4):
            slot, dev = peerx(d)
            mine = pltpu.make_async_remote_copy(
                src_ref=src.at[slot], dst_ref=dst.at[x], send_sem=as_sem.at[n, d], recv_sem=ar_sem.at[n, x],
                device_id=dev, device_id_type=MESH,
            )
            if do == "start":
                mine.start()
            else:
                mine.wait_send()
                pltpu.make_async_remote_copy(
                    src_ref=src.at[slot], dst_ref=dst.at[slot], send_sem=as_sem.at[n, d], recv_sem=ar_sem.at[n, slot],
                    device_id=dev, device_id_type=MESH,
                ).wait_recv()

    def chunks(body, init=None, step=CH):
        def f(i, carry):
            return body(pl.multiple_of(i * step, step), carry)
        return lax.fori_loop(0, R // step, f, init)

    def stats(load):
        zero = jnp.zeros((8, C), F32)
        total = chunks(lambda o, acc: acc + fold(load(o)), zero)
        mean = jnp.sum(total, axis=0, keepdims=True) * (1.0 / R)
        m2 = chunks(lambda o, acc: acc + fold(jnp.square(load(o) - mean)), zero)
        return jnp.concatenate([mean, jnp.sum(m2, axis=0, keepdims=True)], axis=0)

    small[0].wait()
    first = stats(lambda o: seq_ref[pl.ds(o, CH), :].astype(F32))
    tracks = hb_ref.shape[0]

    def prepare_bias():
        small[3].wait()
        hbp[...] = jnp.zeros(hbp.shape, F32)
        last = tracks // Q * Q
        for i in range(tracks // Q):
            hbp[i:i + 1, :] = hb_ref[pl.ds(i * Q, Q)].reshape(1, Q)
        hbp[tracks // Q:tracks // Q + 1, 0:tracks - last] = hb_ref[pl.ds(last, tracks - last)].reshape(1, tracks - last)

        @pl.loop(0, hbp.shape[0] - 6)
        def _(i):
            bcol[pl.ds(pl.multiple_of(i * Q, Q), Q), :] = jnp.broadcast_to(hbp[pl.ds(i, 1), :], (Q, Q)).T

    zeros = jnp.zeros((PAD, C), BF16)
    for buf in (act0, act1, gpad):
        buf[0:PAD] = zeros
        buf[PAD + R:] = zeros
    pl.semaphore_wait(barrier, 31)

    def begin():
        for d in range(1, 4):
            slot, dev = peerx(d)
            pltpu.make_async_remote_copy(
                src_ref=seq_ref.at[pl.ds(pl.multiple_of(slot * Q, Q), Q)], dst_ref=xq.at[x], send_sem=as_sem.at[0, d],
                recv_sem=ar_sem.at[0, x], device_id=dev, device_id_type=MESH,
            ).start()
        xq[x] = seq_ref[pl.ds(pl.multiple_of(x * Q, Q), Q), :]

    def prepare_weights():
        loads[1].wait()
        tracks = wt.shape[0]
        edge = tracks // 256 * 256
        wtail[...] = jnp.zeros(wtail.shape, BF16)
        wtail[0:tracks - edge] = wt[edge:tracks]

        @pl.loop(0, tracks // 256)
        def _(i):
            o = pl.multiple_of(i * 256, 256)
            w[:, pl.ds(o, 256)] = wt[pl.ds(o, 256), :].T
        w[:, edge:edge + 256] = wtail[...].T

    def prepare_counts():
        for cp in loads[2:]:
            cp.wait()
        tracks = tg.shape[0]
        edge = tracks // 256 * 256
        ttail[...] = jnp.zeros(ttail.shape, jnp.int32)
        ttail[0:tracks - edge] = tg[edge:tracks]

    def blocked(ref):
        return lambda o: ref[o // Q, pl.ds(lax.rem(o, Q), CH), :].astype(F32)

    def loader(ref):
        return lambda o: ref[pl.ds(o, CH), :]

    load_x = [blocked(xq), loader(x1), blocked(x2)]
    acts, actTs, gps = [act0, act1, None], [actT0, actT1], [gp0, gp1]
    norms = []

    def norm(k, moments):
        inv = lax.rsqrt(moments[1:2] * (1.0 / (R * NDEV)) + EPS)
        norms.append((moments[0:1], inv, gain_ref[k:k + 1, :], shift_ref[k:k + 1, :]))

    def xhat_at(k, o, load=None):
        mean, inv, _, _ = norms[k]
        return ((load or load_x[k])(o) - mean) * inv

    def pre_at(k, o):
        load = blocked(x2o) if k == 2 else None
        return xhat_at(k, o, load) * norms[k][2] + norms[k][3]

    def activate(k, store):
        def body(o, _):
            pre = pre_at(k, o)
            store(o, (pre * cdf_of(pre)).astype(BF16))
        chunks(body)

    def slopes(k):
        def body(o, _):
            gps[k][pl.ds(o, CH), :] = slope_of(pre_at(k, o))
        chunks(body)

    moments = sync(0, first, True, begin, prepare_weights)
    small[1].wait()
    small[2].wait()
    norm(0, moments)
    a2a(0, xq, xq, "wait")
    loads[0].wait()
    spans = (Q, 2 * Q)
    for l in range(2):
        act, span = acts[l], spans[l]

        def keep(o, v, act=act):
            act[pl.ds(PAD + o, CH), :] = v

        activate(l, keep)
        for r in range(0, R, 256):
            acc = nn(act[pl.ds(PAD - span + r, 256), :], cw[l, 0])
            acc += nn(act[pl.ds(PAD + r, 256), :], cw[l, 1])
            acc += nn(act[pl.ds(PAD + span + r, 256), :], cw[l, 2])
            if l == 0:
                old = jnp.concatenate([xq[r // Q], xq[r // Q + 1]], axis=0).astype(F32)
            else:
                old = x1[pl.ds(r, 256), :]
            new = old + acc
            if l == 0:
                x1[pl.ds(r, 256), :] = new
            else:
                x2[r // Q] = new[0:Q]
                x2[r // Q + 1] = new[Q:2 * Q]

        def side(l=l, act=act):
            if l == 1:
                a2a(1, x2, x2o, "start")
                x2o[x] = x2[x]
            slopes(l)
            actTs[l][...] = act[pl.ds(PAD, R), :].T

        moments = sync(l + 1, stats(load_x[l + 1]), True, side, (prepare_bias, prepare_counts)[l])
        norm(l + 1, moments)

    full = tracks // TW
    rest = tracks - full * TW
    tiles = full + 1
    half = C // 2
    other = (dp, sq + 1 - 2 * core)

    def rcopy(src, dst, ssem, rsem, dev):
        return pltpu.make_async_remote_copy(
            src_ref=src, dst_ref=dst, send_sem=ssem, recv_sem=rsem, device_id=dev, device_id_type=MESH
        )

    def keep_h(o, v):
        h[o // Q, pl.ds(lax.rem(o, Q), CH), :] = v

    a2a(1, x2, x2o, "wait")
    activate(2, keep_h)
    for k in range(4):
        part = h[k].T
        hT[:, k * Q:(k + 1) * Q] = part
        wide = part.astype(F32)
        for s in range(16):
            sx, sz, sc = s // 4, (s // 2) % 2, s % 2
            to = jnp.where(core == sc, half, 0) + sx * 48 + sz * 24
            dhacc[pl.ds(pl.multiple_of(to, 8), 24), k * Q:(k + 1) * Q] = wide[24 * s:24 * s + 24]
    hPb[0:C] = dhacc[...].astype(BF16)
    ones_row = lax.broadcasted_iota(jnp.int32, (16, R), 0) == 0
    hPb[C:C + 16] = jnp.where(ones_row, 1.0, 0.0).astype(BF16)
    scale = 1.0 / math.sqrt(R * NDEV)

    def piece(rows, counts, bias, at, live):
        v = nn(rows, hT[...])
        for j in range(4):
            z = v[:, j * Q:(j + 1) * Q] + bias
            e = (jnp.exp(z) - counts[:, j * Q:(j + 1) * Q].astype(F32)) * scale
            if live is not None:
                e = jnp.where(lax.broadcasted_iota(jnp.int32, e.shape, 0) < live, e, 0.0)
            dz[at:at + 256, j * Q:(j + 1) * Q] = e.astype(BF16)

    def tile(t, start, tail, turn):
        for i in range(3):
            o = start + i * 256 if tail else pl.multiple_of(start + i * 256, 256)
            if tail and i == 2:
                piece(wtail[...], ttail[...], bcol[pl.ds(o, 256), :], i * 256, rest - 512)
            else:
                piece(wt[pl.ds(o, 256), :], tg[pl.ds(o, 256), :], bcol[pl.ds(o, 256), :], i * 256, None)
        part = nt(hPb[...], dz[...])
        gsend[t] = part[0:half].astype(BF16)
        gown[turn] = part[half:C]
        bb1[0, me1, pl.ds(t, 1), :] = part[C:C + 1]
        add = nn(w[:, pl.ds(start if tail else pl.multiple_of(start, TW), TW)], dz[...])
        dhacc[...] += add
        rcopy(gsend.at[t], grecv.at[t], gcs.at[t], gcr.at[t], other).start()

    def chip(t, slot):
        rcopy(gsend.at[t], grecv.at[t], gcs.at[t], gcr.at[t], other).wait()
        for k in range(4):
            xsend[t, k] = (gown[slot, k * 48:(k + 1) * 48] + grecv[t, k * 48:(k + 1) * 48].astype(F32)).astype(BF16)

    def xstart(t):
        for d in range(1, 4):
            slot, dev = peerx(d)
            rcopy(xsend.at[t, slot], xrecv.at[t, x], gxs.at[t, slot], gxr.at[t, x], dev).start()

    def owner(t, i):
        return t, x * 4 + i * 2 + core

    def yz(t, i):
        return rcopy(ysend.at[t, i], yrecv.at[me2], gys.at[t, i], gyr.at[me2], owner(t, i))

    def spread_rows(t, total):
        for i in range(2):
            ysend[t, i] = total[i * 24:i * 24 + 24].astype(BF16)

            @pl.when(jnp.logical_or(dp != t, zl != i))
            def _(i=i):
                yz(t, i).start()

    def ystart(t):
        total = xsend[t, x].astype(F32)
        for d in range(1, 4):
            slot, dev = peerx(d)
            rcopy(xsend.at[t, slot], xrecv.at[t, slot], gxs.at[t, slot], gxr.at[t, slot], dev).wait()
            total = total + xrecv[t, slot].astype(F32)
        spread_rows(t, total)

    def vstart(t):
        @pl.when(y != t)
        def _():
            rcopy(xsend.at[t], vrecv.at[y], hvs.at[t], hvr.at[y], (zh * 4 + t, sq)).start()

    def vmid():
        for d in range(1, 4):
            slot, dev = peery(d)
            rcopy(vrecv.at[slot], vrecv.at[slot], hvs.at[slot], hvr.at[slot], dev).wait_recv()
        for k in range(4):
            total = xsend[y, k].astype(F32)
            for d in range(1, 4):
                total = total + vrecv[lax.rem(y + d, 4), k].astype(F32)
            vsend[k] = total.astype(BF16)
        for d in range(1, 4):
            slot, dev = peerx(d)
            rcopy(vsend.at[slot], vx.at[x], hxs.at[slot], hxr.at[x], dev).start()

    def vend():
        total = vsend[x].astype(F32)
        for d in range(1, 4):
            slot, dev = peerx(d)
            rcopy(vsend.at[slot], vx.at[slot], hxs.at[slot], hxr.at[slot], dev).wait()
            total = total + vx[slot].astype(F32)
        spread_rows(y, total)
        for d in range(1, 4):
            slot, dev = peery(d)
            rcopy(xsend.at[slot], vrecv.at[slot], hvs.at[slot], hvr.at[slot], dev).wait_send()

    def finish_head():
        @pl.when(dp < tiles)
        def _():
            near = dp < 4

            def body(d, total):
                slot = jnp.where(near, y * 4 + lax.rem(me2 + d, 4), lax.rem(me2 + d, 16))
                rcopy(yrecv.at[slot], yrecv.at[slot], gys.at[0, 0], gyr.at[slot], dev2(slot)).wait_recv()
                return total + yrecv[slot].astype(F32)
            total = lax.fori_loop(1, jnp.where(near, 4, 16), body, ysend[dp, zl].astype(F32))
            fall[dp] = total.astype(BF16)

            @pl.loop(1, 8)
            def _(d):
                slot = lax.rem(dp + d, 8)
                rcopy(fall.at[dp], fall.at[dp], gfs.at[slot], gfr.at[dp], (slot, sq)).start()

    def collect_head():
        @pl.loop(0, tiles)
        def _(t):
          @pl.when(jnp.logical_or(t >= 4, t == y))
          def _():
            for i in range(2):
                @pl.when(jnp.logical_or(dp != t, zl != i))
                def _(i=i):
                    yz(t, i).wait_send()

        @pl.when(dp < tiles)
        def _():
            @pl.loop(1, 8)
            def _(d):
                slot = lax.rem(dp + d, 8)
                rcopy(fall.at[dp], fall.at[dp], gfs.at[slot], gfr.at[dp], (slot, sq)).wait_send()

        for t in range(tiles):
            @pl.when(dp != t)
            def _(t=t):
                rcopy(fall.at[t], fall.at[t], gfs.at[0], gfr.at[t], (t, sq)).wait_recv()
        for t in range(full):
            ghead_ref[:, t * TW:(t + 1) * TW] = fall[t].astype(F32)
        ghead_ref[:, full * TW:tracks] = fall[full].astype(F32)[:, 0:rest]
        pltpu.make_async_copy(ghead_ref, ghead_hbm, out_sem.at[1]).start()

    def bias_start():
        exchange(bb1, 0, me1, 8, peer1, e1_sem, q1_sem, "start")

    def bias_row(t):
        return rcopy(brow.at[t], bin_.at[me2], brs.at[t], brr.at[me2], dev2(t))

    def bias_middle():
        exchange(bb1, 0, me1, 8, peer1, e1_sem, q1_sem, "wait")
        total = functools.reduce(lambda a, b: a + b, [bb1[0, i] for i in range(8)])
        for t in range(tiles):
            brow[t] = total[t:t + 1]

            @pl.when(me2 != t)
            def _(t=t):
                bias_row(t).start()

    def bias_own():
        @pl.when(me2 < tiles)
        def _():
            def body(d, total):
                slot, dev = peer2(d)
                rcopy(bin_.at[slot], bin_.at[slot], brs.at[0], brr.at[slot], dev).wait_recv()
                return total + bin_[slot]
            ball[me2] = lax.fori_loop(1, 16, body, brow[me2])

            @pl.loop(1, 16)
            def _(d):
                slot, dev = peer2(d)
                rcopy(ball.at[me2], ball.at[me2], e2_sem.at[slot], q2_sem.at[me2], dev).start()

    def bias_end():
        for t in range(tiles):
            n = min(TW, tracks - t * TW)

            @pl.when(me2 != t)
            def _(t=t):
                bias_row(t).wait_send()
                rcopy(ball.at[t], ball.at[t], e2_sem.at[0], q2_sem.at[t], dev2(t)).wait_recv()
            gbias_ref[pl.ds(t * TW, n)] = ball[t][0, 0:n]

        @pl.when(me2 < tiles)
        def _():
            @pl.loop(1, 16)
            def _(d):
                slot, dev = peer2(d)
                rcopy(ball.at[me2], ball.at[me2], e2_sem.at[slot], q2_sem.at[me2], dev).wait_send()

    dhacc[...] = jnp.zeros(dhacc.shape, F32)

    def near(i):
        return lax.rem(y + 1 + i, 4)

    @pl.loop(0, 3)
    def _(i):
        tile(near(i), near(i) * TW, False, i % 2)

        @pl.when(i > 0)
        def _():
            chip(near(i - 1), (i + 1) % 2)
            vstart(near(i - 1))

    tile(full, full * TW, True, 1)
    chip(near(2), 0)
    vstart(near(2))

    @pl.loop(0, 3)
    def _(i):
        t = jnp.where(i == 0, 4, jnp.where(i == 1, y, 5))
        tile(t, t * TW, False, i % 2)
        chip(jnp.where(i == 0, full, jnp.where(i == 1, 4, y)), (i + 1) % 2)

        @pl.when(i == 0)
        def _():
            xstart(full)

    chip(5, 0)

    class Job:
        def __init__(self, number, layer, taps, at, ring, me, peer, dev):
            self.q, self.layer, self.taps, self.at, self.ring = number, layer, taps, at, ring
            self.me, self.peer, self.dev, self.owners = me, peer, dev, 3 * len(taps)

    jobs = (
        Job(0, 1, (0, 1, 2), y, peery, me3, peer3, dev3),
        Job(1, 0, (0, 2), x, peerx, me2, peer2, dev2),
        Job(2, 0, (1,), y, peery, me3, peer3, dev3),
    )

    def conv_start(l, span, actT, taps):
        for j in taps:
            cfull[j] = nn(actT[...], gpad[pl.ds(PAD + (1 - j) * span, R), :])
            csend[l, j] = cfull[j, pl.ds(pl.multiple_of((1 - core) * half, 64), half), :].astype(BF16)
            rcopy(csend.at[l, j], crecv.at[l, j], ccs.at[l, j], ccr.at[l, j], other).start()

    def conv_x(job):
        l, q = job.layer, job.q
        for i, j in enumerate(job.taps):
            rcopy(csend.at[l, j], crecv.at[l, j], ccs.at[l, j], ccr.at[l, j], other).wait()
            for k in range(4):
                mine = cfull[j, pl.ds(pl.multiple_of(core * half + k * 48, 16), 48), :]
                cx[q, i, k] = (mine + crecv[l, j, k * 48:(k + 1) * 48].astype(F32)).astype(BF16)
            for d in range(1, 4):
                slot, dev = job.ring(d)
                rcopy(cx.at[q, i, slot], cxr.at[q, i, job.at], cxs.at[q, i, slot], cxrs.at[q, i, job.at], dev).start()

    def block(job, i):
        q, me = job.q, job.me
        return rcopy(cy.at[q, i], cyr.at[q, me], cys.at[q, i], cyrs.at[q, me], job.dev(i))

    def conv_rs(job):
        q = job.q
        for j in range(len(job.taps)):
            total = cx[q, j, job.at].astype(F32)
            for d in range(1, 4):
                slot, dev = job.ring(d)
                rcopy(cx.at[q, j, slot], cxr.at[q, j, slot], cxs.at[q, j, slot], cxrs.at[q, j, slot], dev).wait()
                total = total + cxr[q, j, slot].astype(F32)
            for b in range(3):
                i = 3 * j + b
                cy[q, i] = total[b * 16:(b + 1) * 16].astype(BF16)

                @pl.when(job.me != i)
                def _(i=i):
                    block(job, i).start()

    def piece_of(job):
        return cz.at[job.q, job.me // 3, job.me % 3]

    def conv_ag(job):
        q = job.q

        @pl.when(job.me < job.owners)
        def _():
            def body(d, total):
                slot, dev = job.peer(d)
                rcopy(cyr.at[q, slot], cyr.at[q, slot], cys.at[q, 0], cyrs.at[q, slot], dev).wait_recv()
                return total + cyr[q, slot].astype(F32)
            total = lax.fori_loop(1, 16, body, cy[q, job.me].astype(F32))
            cz[q, job.me // 3, job.me % 3] = total.astype(BF16)

            @pl.loop(1, 16)
            def _(d):
                slot, dev = job.peer(d)
                rcopy(piece_of(job), piece_of(job), czs.at[q, slot], czrs.at[q, job.me], dev).start()

    def conv_xag(job):
        q = job.q
        for j in range(len(job.taps)):
            for b in range(3):
                i = 3 * j + b

                @pl.when(job.me != i)
                def _(i=i, j=j, b=b):
                    rcopy(cz.at[q, j, b], cz.at[q, j, b], czs.at[q, 0], czrs.at[q, i], job.dev(i)).wait_recv()
            for d in range(1, 4):
                slot, dev = job.ring(d)
                rcopy(cz.at[q, j], ca.at[q, j, job.at], cas.at[q, j, slot], cars.at[q, j, job.at], dev).start()
            ca[q, j, job.at] = cz[q, j]

    def put(job, i, side):
        src = (ca, cb)[side].at[job.q, i]
        at = 1 - core if side else core
        return pltpu.make_async_copy(src, gconv_hbm.at[job.layer, job.taps[i], at], oc_sem.at[job.q, i, side])

    def conv_cag(job):
        q = job.q
        for i, j in enumerate(job.taps):
            for d in range(1, 4):
                slot, dev = job.ring(d)
                rcopy(cz.at[q, i], ca.at[q, i, slot], cas.at[q, i, slot], cars.at[q, i, slot], dev).wait()
            rcopy(ca.at[q, i], cb.at[q, i], cbs.at[q, i], cbrs.at[q, i], other).start()
            put(job, i, 0).start()

    def conv_end(job):
        q = job.q
        for i, j in enumerate(job.taps):
            rcopy(ca.at[q, i], cb.at[q, i], cbs.at[q, i], cbrs.at[q, i], other).wait()
            put(job, i, 1).start()
        for i in range(job.owners):
            @pl.when(job.me != i)
            def _(i=i):
                block(job, i).wait_send()

        @pl.when(job.me < job.owners)
        def _():
            @pl.loop(1, 16)
            def _(d):
                slot, dev = job.peer(d)
                rcopy(piece_of(job), piece_of(job), czs.at[q, slot], czrs.at[q, job.me], dev).wait_send()

    n = float(R * NDEV)

    def sums(k, load):
        def body(o, acc):
            v = load(o) * gps[k][pl.ds(o, CH), :]
            dpre[pl.ds(o, CH), :] = v
            return acc[0] + fold(v), acc[1] + fold(v * xhat_at(k, o))
        zero = jnp.zeros((8, C), F32)
        a, b = chunks(body, (zero, zero))
        return jnp.concatenate([jnp.sum(a, axis=0, keepdims=True), jnp.sum(b, axis=0, keepdims=True)], axis=0)

    def report(k, s):
        gshift_ref[k:k + 1, :] = s[0:1]
        ggain_ref[k:k + 1, :] = s[1:2]

    def dv_at(k, o, s):
        _, inv, gain, _ = norms[k]
        v = blocked(dpq)(o) if k == 2 else dpre[pl.ds(o, CH), :]
        return gain * inv * (v - s[0:1] * (1.0 / n) - xhat_at(k, o) * (s[1:2] * (1.0 / n)))

    def back(o, acc):
        k = o // Q
        v = dpre[pl.ds(o, CH), :] * slope_of(pre_at(2, o))
        dps[k, pl.ds(lax.rem(o, Q), CH), :] = v.astype(BF16)
        return acc[0] + fold(v), acc[1] + fold(v * xhat_at(2, o, blocked(x2o)))

    for k in range(4):
        dpre[k * Q:(k + 1) * Q] = dhacc[:, k * Q:(k + 1) * Q].T
    zero = jnp.zeros((8, C), F32)
    left, right = chunks(back, (zero, zero))
    value = jnp.concatenate([jnp.sum(left, axis=0, keepdims=True), jnp.sum(right, axis=0, keepdims=True)], axis=0)

    def fill31():
        bias_start()
        a2a(2, dps, dpq, "start")
        dpq[x] = dps[x]
        xstart(4)
        xstart(5)

    def fill32():
        bias_middle()
        ystart(full)

    s = sync(3, value, False, fill31, fill32)
    report(2, s)
    a2a(2, dps, dpq, "wait")

    for l in (1, 0):
        span = spans[l]

        def spread(o, _, l=l, s=s):
            v = dv_at(l + 1, o, s)
            if l == 0:
                v = v + g[pl.ds(o, CH), :]
            g[pl.ds(o, CH), :] = v
            gpad[pl.ds(PAD + o, CH), :] = v.astype(BF16)

        chunks(spread)
        if l == 0:
            conv_start(0, span, actTs[0], (0, 1, 2))
        for r in range(0, R, 256):
            acc = nt(gpad[pl.ds(PAD + span + r, 256), :], cw[l, 0])
            acc += nt(gpad[pl.ds(PAD + r, 256), :], cw[l, 1])
            acc += nt(gpad[pl.ds(PAD - span + r, 256), :], cw[l, 2])
            dpre[pl.ds(r, 256), :] = acc

        if l == 0:
            conv_x(jobs[1])
            conv_x(jobs[2])
        value = sums(l, lambda o: dpre[pl.ds(o, CH), :])

        def early(l=l, span=span):
            if l == 0:
                conv_rs(jobs[0])
                _, inv, gain, _ = norms[0]

                def body(o, _):
                    v = g[pl.ds(o, CH), :] + gain * inv * dpre[pl.ds(o, CH), :]
                    asend[o // Q, pl.ds(lax.rem(o, Q), CH), :] = v.astype(BF16)
                chunks(body)
                conv_rs(jobs[2])
                conv_rs(jobs[1])
                a2a(3, asend, arecv, "start")
                arecv[x] = asend[x]
            else:
                conv_start(1, span, actTs[1], (0, 1, 2))
                vmid()

        def late(l=l):
            if l == 1:
                conv_x(jobs[0])
                ystart(4)
                ystart(5)
                vend()
                bias_own()
            else:
                conv_ag(jobs[2])
                conv_ag(jobs[1])
                conv_ag(jobs[0])
                finish_head()

        s = sync(5 - l, value, False, early, late)
        report(l, s)

    a2a(3, asend, arecv, "wait")
    mean, inv, gain, _ = norms[0]

    def finish(o, _):
        xh = (seq_ref[pl.ds(o, CH), :].astype(F32) - mean) * inv
        part = blocked(arecv)(o)
        g[pl.ds(o, CH), :] = part - gain * inv * (s[0:1] * (1.0 / n) + xh * (s[1:2] * (1.0 / n)))
    chunks(finish)
    put_in = pltpu.make_async_copy(g, gin_hbm, out_sem.at[0])
    put_in.start()
    conv_xag(jobs[2])
    conv_xag(jobs[1])
    conv_xag(jobs[0])
    bias_end()
    collect_head()
    conv_cag(jobs[2])
    conv_cag(jobs[1])
    conv_cag(jobs[0])
    conv_end(jobs[2])
    conv_end(jobs[1])
    conv_end(jobs[0])
    put_in.wait()
    pltpu.make_async_copy(ghead_ref, ghead_hbm, out_sem.at[1]).wait()
    for job in jobs:
        for i in range(len(job.taps)):
            put(job, i, 0).wait()
            put(job, i, 1).wait()


def emit(gin, ggain, gshift, ghead, gbias, gconv, *rest):
    outs, bufs, wide, isem, osem = rest[:6], rest[6:12], rest[12], rest[13], rest[14]
    ins = [pltpu.make_async_copy(src, dst, isem.at[i]) for i, (src, dst) in
           enumerate(zip((gin, ggain, gshift, ghead, gbias), bufs))]
    taps = [pltpu.make_async_copy(gconv.at[j], bufs[5].at[j], isem.at[5 + j]) for j in range(6)]
    for cp in taps + ins:
        cp.start()
    back = [pltpu.make_async_copy(src, dst, osem.at[i]) for i, (src, dst) in
            enumerate(zip(bufs, (outs[0], outs[2], outs[3], outs[4], outs[5])))]
    send = [pltpu.make_async_copy(wide.at[j], outs[1].at[j], osem.at[5 + j]) for j in range(6)]
    for j in range(6):
        taps[j].wait()
        wide[j] = bufs[5][j].astype(F32)
        send[j].start()
    for a, b in zip(ins, back):
        a.wait()
        b.start()
    for cp in send + back:
        cp.wait()


def on_device(sequence, conv_weight, gains, shifts, head_weight, head_bias, targets):
    tracks = head_weight.shape[1]
    vmem = pl.BlockSpec(memory_space=pltpu.VMEM)
    hbm = pl.BlockSpec(memory_space=pl.ANY)
    sds = jax.ShapeDtypeStruct
    V = pltpu.VMEM
    D = pltpu.SemaphoreType.DMA
    T7 = tracks // TW + 1
    W7 = T7 * TW
    gin, ggain, gshift, ghead, gbias, gconv = pl.pallas_call(
        kernel,
        out_shape=(
            sds((R, C), F32), sds((3, C), F32), sds((3, C), F32), sds((C // 16, tracks), F32), sds((tracks,), F32),
            sds((2, 3, 2, 4, 3, 16, C), BF16),
        ),
        in_specs=[hbm] * 7,
        out_specs=(hbm, vmem, vmem, hbm, vmem, hbm),
        scratch_shapes=[
            V((R, C), BF16), V((3, C), F32), V((3, C), F32), V((tracks,), F32), V((C // 16, tracks), F32),
            V((2, 3, C, C), BF16), V((tracks, C), BF16), V((256, C), BF16), V((C, W7), BF16),
            V((tracks, R), jnp.int32), V((256, R), jnp.int32), V((W7, Q), F32), V((48, Q), F32),
            V((4, Q, C), BF16), V((R, C), F32), V((4, Q, C), F32), V((4, Q, C), F32),
            V((R + 2 * PAD, C), BF16), V((R + 2 * PAD, C), BF16), V((C, R), BF16), V((C, R), BF16),
            V((C, R), BF16), V((C + 16, R), BF16), V((TW, R), BF16),
            V((C, R), F32), V((4, Q, C), BF16), V((4, Q, C), BF16),
            V((R, C), F32), V((R, C), F32), V((R + 2 * PAD, C), BF16), V((R, C), F32), V((R, C), F32),
            V((4, Q, C), BF16),
            V((6, 8, 2, C), F32), V((6, 16, 2, C), F32), V((1, 8, 8, TW), F32), V((8, 1, TW), F32), V((16, 1, TW), F32), V((8, 1, TW), F32),
            V((T7, 192, TW), BF16), V((T7, 192, TW), BF16), V((2, 192, TW), F32),
            V((T7, 4, 48, TW), BF16), V((T7, 4, 48, TW), BF16), V((T7, 2, 24, TW), BF16), V((16, 24, TW), BF16), V((T7, 24, TW), BF16),
            V((4, 4, 48, TW), BF16), V((4, 48, TW), BF16), V((4, 48, TW), BF16),
            V((3, C, C), F32), V((2, 3, C // 2, C), BF16), V((2, 3, C // 2, C), BF16), V((3, 3, 4, 48, C), BF16),
            V((3, 3, 4, 48, C), BF16), V((3, 9, 16, C), BF16), V((3, 16, 16, C), BF16), V((3, 3, 3, 16, C), BF16),
            V((3, 3, 4, 3, 16, C), BF16), V((3, 3, 4, 3, 16, C), BF16),
            D((10,)), D((8,)), D((16,)), D((6, 8)), D((6, 16)), D((4, 4)), D((4, 4)),
            D((8,)), D((16,)), D((1, 8)), D((8,)), D((8,)), D((16,)), D((T7,)), D((T7,)), D((T7, 4)), D((T7, 4)), D((T7, 2)), D((16,)),
            D((8,)), D((T7,)), D((4,)), D((4,)), D((4,)), D((4,)),
            D((2,)), D((3, 3, 2)), D((2, 3)), D((2, 3)), D((3, 3, 4)), D((3, 3, 4)), D((3, 9)), D((3, 16)), D((3, 16)), D((3, 9)), D((3, 3, 4)), D((3, 3, 4)),
            D((3, 3)), D((3, 3)),
        ],
        compiler_params=pltpu.CompilerParams(
            collective_id=0, has_side_effects=True, vmem_limit_bytes=67043328
        ),
        name="whole",
    )(sequence.reshape(R, C), gains, shifts, head_bias, conv_weight, head_weight.T, jnp.transpose(targets, (2, 0, 1)))
    gin, grad_conv, ggain, gshift, ghead, gbias = pl.pallas_call(
        emit,
        out_shape=(
            sds((R, C), F32), sds((6, C, C), F32), sds((3, C), F32), sds((3, C), F32), sds((C // 16, tracks), F32),
            sds((tracks,), F32),
        ),
        in_specs=[hbm] * 6,
        out_specs=(hbm,) * 6,
        scratch_shapes=[
            V((R, C), F32), V((3, C), F32), V((3, C), F32), V((C // 16, tracks), F32), V((tracks,), F32),
            V((6, C, C), BF16), V((6, C, C), F32), D((11,)), D((11,)),
        ],
        name="emit",
    )(gin, ggain, gshift, ghead, gbias, gconv.reshape(6, C, C))
    return gin.reshape(1, R, C), grad_conv.reshape(2, 3, C, C), ggain, gshift, ghead, gbias


def solution(mesh):
    rep = P()
    return jax.shard_map(
        on_device,
        mesh=mesh,
        in_specs=(P("dp", "seq", None), rep, rep, rep, rep, rep, P("dp", "seq", None)),
        out_specs=(P("dp", "seq", None), rep, rep, rep, P("seq", None), rep),
        check_vma=False,
    )
```

```python
import functools
import math

import jax
import jax.numpy as jnp
from jax import lax
from jax.experimental import pallas as pl
from jax.experimental.pallas import tpu as pltpu
from jax.sharding import PartitionSpec as P

MESH = pl.DeviceIdType.MESH
F32 = jnp.float32
BF16 = jnp.bfloat16
EPS = 1e-05
C = 384
R = 512
Q = 128
TW = 768
CH = 32
PAD = 256
NDEV = 128


def nn(a, b):
    return lax.dot_general(a, b, (((1,), (0,)), ((), ())), preferred_element_type=F32)


def nt(a, b):
    return lax.dot_general(a, b, (((1,), (1,)), ((), ())), preferred_element_type=F32)


def fold(v):
    return v.reshape(v.shape[0] // 8, 8, v.shape[1]).sum(axis=0)


def cdf_of(pre):
    return 0.5 * (1.0 + lax.erf(pre * math.sqrt(0.5)))


def slope_of(pre):
    return cdf_of(pre) + pre * (jnp.exp(-0.5 * pre * pre) * (1.0 / math.sqrt(2.0 * math.pi)))


def kernel(
    seq_hbm, gain_hbm, shift_hbm, hb_hbm, cw_hbm, hw_hbm, tg_hbm,
    gin_hbm, ggain_ref, gshift_ref, ghead_hbm, gbias_ref, gconv_hbm,
    seq_ref, gain_ref, shift_ref, hb_ref, ghead_ref,
    cw, wt, wtail, w, tg, ttail, bcol, hbp, xq, x1, x2, x2o, act0, act1, actT0, actT1, hT, hPb, dz, dhacc, dps, dpq,
    gp0, gp1, gpad, g, dpre, arecv, b1, b2, bb1, brow, bin_, ball,
    gsend, grecv, gown, xsend, xrecv, ysend, yrecv, fall, vrecv, vsend, vx,
    cfull, csend, crecv, cx, cxr, cy, cyr, cz, ca, cb,
    load_sem, s1_sem, s2_sem, r1_sem, r2_sem, as_sem, ar_sem,
    e1_sem, e2_sem, q1_sem, q2_sem, brs, brr, gcs, gcr, gxs, gxr, gys, gyr, gfs, gfr, hvs, hvr, hxs, hxr,
    out_sem, oc_sem, ccs, ccr, cxs, cxrs, cys, cyrs, czs, czrs, cas, cars, cbs, cbrs,
):
    h = asend = dps
    dp = lax.axis_index("dp")
    sq = lax.axis_index("seq")
    x, zl, core = sq // 4, (sq // 2) % 2, sq % 2
    zh, y = dp // 4, dp % 4
    me1 = x * 2 + core
    me2 = y * 4 + zh * 2 + zl
    me3 = x * 4 + zh * 2 + zl

    def peer1(d):
        slot = lax.rem(me1 + d, 8)
        return slot, (dp, (slot // 2) * 4 + zl * 2 + slot % 2)

    def peer2(d):
        slot = lax.rem(me2 + d, 16)
        return slot, (((slot // 2) % 2) * 4 + slot // 4, x * 4 + (slot % 2) * 2 + core)

    def peerx(d):
        slot = lax.rem(x + d, 4)
        return slot, (dp, slot * 4 + zl * 2 + core)

    def peery(d):
        slot = lax.rem(y + d, 4)
        return slot, (zh * 4 + slot, sq)

    def dev2(i):
        return ((i // 2) % 2) * 4 + i // 4, x * 4 + (i % 2) * 2 + core

    def dev3(i):
        return ((i // 2) % 2) * 4 + y, (i // 4) * 4 + (i % 2) * 2 + core

    def peer3(d):
        slot = lax.rem(me3 + d, 16)
        return slot, dev3(slot)

    barrier = pltpu.get_barrier_semaphore()

    @pl.loop(0, 9)
    def _(i):
        slot = lax.rem(x + 1 + i // 3, 4) * 4 + lax.rem(zh * 2 + zl + 1 + i % 3, 4)
        pl.semaphore_signal(barrier, inc=1, device_id=dev3(slot), device_id_type=MESH)

    @pl.loop(1, 8)
    def _(d):
        pl.semaphore_signal(barrier, inc=1, device_id=peer1(d)[1], device_id_type=MESH)

    @pl.loop(1, 16)
    def _(d):
        pl.semaphore_signal(barrier, inc=1, device_id=peer2(d)[1], device_id_type=MESH)

    small = [
        pltpu.make_async_copy(src, dst, load_sem.at[6 + i])
        for i, (src, dst) in enumerate(((seq_hbm, seq_ref), (gain_hbm, gain_ref), (shift_hbm, shift_ref), (hb_hbm, hb_ref)))
    ]
    loads = [
        pltpu.make_async_copy(cw_hbm, cw, load_sem.at[0]),
        pltpu.make_async_copy(hw_hbm, wt, load_sem.at[1]),
    ] + [
        pltpu.make_async_copy(tg_hbm.at[:, 0, j * Q:(j + 1) * Q], tg.at[:, j * Q:(j + 1) * Q], load_sem.at[2 + j])
        for j in range(4)
    ]
    for cp in small + loads:
        cp.start()

    def exchange(buf, k, me, count, peer, ssem, rsem, do):
        def cp(d):
            slot, dev = peer(d)
            return slot, dev

        if do == "start":
            @pl.loop(1, count)
            def _(d):
                slot, dev = peer(d)
                pltpu.make_async_remote_copy(
                    src_ref=buf.at[k, me], dst_ref=buf.at[k, me], send_sem=ssem.at[slot], recv_sem=rsem.at[k, me],
                    device_id=dev, device_id_type=MESH,
                ).start()
        else:
            @pl.loop(1, count)
            def _(d):
                slot, dev = peer(d)
                pltpu.make_async_remote_copy(
                    src_ref=buf.at[k, me], dst_ref=buf.at[k, slot], send_sem=ssem.at[slot], recv_sem=rsem.at[k, slot],
                    device_id=dev, device_id_type=MESH,
                ).wait()

    def merge(buf, k, count, each, forward):
        parts = [buf[k, i] for i in range(count)]
        total = functools.reduce(lambda a, b: a + b, parts)
        if not forward:
            return total
        mean = total[0:1] * (1.0 / count)
        dev = functools.reduce(lambda a, b: a + b, [jnp.square(p[0:1] - mean) for p in parts])
        return jnp.concatenate([mean, total[1:2] + each * dev], axis=0)

    def sync(k, value, forward, work1=None, work2=None):
        b1[k, me1] = value
        exchange(b1, k, me1, 8, peer1, s1_sem, r1_sem, "start")
        if work1 is not None:
            work1()
        exchange(b1, k, me1, 8, peer1, s1_sem, r1_sem, "wait")
        b2[k, me2] = merge(b1, k, 8, float(R), forward)
        exchange(b2, k, me2, 16, peer2, s2_sem, r2_sem, "start")
        if work2 is not None:
            work2()
        exchange(b2, k, me2, 16, peer2, s2_sem, r2_sem, "wait")
        return merge(b2, k, 16, float(R * 8), forward)

    def a2a(n, src, dst, do):
        for d in range(1, 4):
            slot, dev = peerx(d)
            mine = pltpu.make_async_remote_copy(
                src_ref=src.at[slot], dst_ref=dst.at[x], send_sem=as_sem.at[n, d], recv_sem=ar_sem.at[n, x],
                device_id=dev, device_id_type=MESH,
            )
            if do == "start":
                mine.start()
            else:
                mine.wait_send()
                pltpu.make_async_remote_copy(
                    src_ref=src.at[slot], dst_ref=dst.at[slot], send_sem=as_sem.at[n, d], recv_sem=ar_sem.at[n, slot],
                    device_id=dev, device_id_type=MESH,
                ).wait_recv()

    def chunks(body, init=None, step=CH):
        def f(i, carry):
            return body(pl.multiple_of(i * step, step), carry)
        return lax.fori_loop(0, R // step, f, init)

    def stats(load):
        zero = jnp.zeros((8, C), F32)
        total = chunks(lambda o, acc: acc + fold(load(o)), zero)
        mean = jnp.sum(total, axis=0, keepdims=True) * (1.0 / R)
        m2 = chunks(lambda o, acc: acc + fold(jnp.square(load(o) - mean)), zero)
        return jnp.concatenate([mean, jnp.sum(m2, axis=0, keepdims=True)], axis=0)

    small[0].wait()
    first = stats(lambda o: seq_ref[pl.ds(o, CH), :].astype(F32))
    tracks = hb_ref.shape[0]

    def prepare_bias():
        small[3].wait()
        hbp[...] = jnp.zeros(hbp.shape, F32)
        last = tracks // Q * Q
        for i in range(tracks // Q):
            hbp[i:i + 1, :] = hb_ref[pl.ds(i * Q, Q)].reshape(1, Q)
        hbp[tracks // Q:tracks // Q + 1, 0:tracks - last] = hb_ref[pl.ds(last, tracks - last)].reshape(1, tracks - last)

        @pl.loop(0, hbp.shape[0] - 6)
        def _(i):
            bcol[pl.ds(pl.multiple_of(i * Q, Q), Q), :] = jnp.broadcast_to(hbp[pl.ds(i, 1), :], (Q, Q)).T

    zeros = jnp.zeros((PAD, C), BF16)
    for buf in (act0, act1, gpad):
        buf[0:PAD] = zeros
        buf[PAD + R:] = zeros
    pl.semaphore_wait(barrier, 31)

    def begin():
        for d in range(1, 4):
            slot, dev = peerx(d)
            pltpu.make_async_remote_copy(
                src_ref=seq_ref.at[pl.ds(pl.multiple_of(slot * Q, Q), Q)], dst_ref=xq.at[x], send_sem=as_sem.at[0, d],
                recv_sem=ar_sem.at[0, x], device_id=dev, device_id_type=MESH,
            ).start()
        xq[x] = seq_ref[pl.ds(pl.multiple_of(x * Q, Q), Q), :]

    def prepare_weights():
        loads[1].wait()
        tracks = wt.shape[0]
        edge = tracks // 256 * 256
        wtail[...] = jnp.zeros(wtail.shape, BF16)
        wtail[0:tracks - edge] = wt[edge:tracks]

        @pl.loop(0, tracks // 256)
        def _(i):
            o = pl.multiple_of(i * 256, 256)
            w[:, pl.ds(o, 256)] = wt[pl.ds(o, 256), :].T
        w[:, edge:edge + 256] = wtail[...].T

    def prepare_counts():
        for cp in loads[2:]:
            cp.wait()
        tracks = tg.shape[0]
        edge = tracks // 256 * 256
        ttail[...] = jnp.zeros(ttail.shape, jnp.int32)
        ttail[0:tracks - edge] = tg[edge:tracks]

    def blocked(ref):
        return lambda o: ref[o // Q, pl.ds(lax.rem(o, Q), CH), :].astype(F32)

    def loader(ref):
        return lambda o: ref[pl.ds(o, CH), :]

    load_x = [blocked(xq), loader(x1), blocked(x2)]
    acts, actTs, gps = [act0, act1, None], [actT0, actT1], [gp0, gp1]
    norms = []

    def norm(k, moments):
        inv = lax.rsqrt(moments[1:2] * (1.0 / (R * NDEV)) + EPS)
        norms.append((moments[0:1], inv, gain_ref[k:k + 1, :], shift_ref[k:k + 1, :]))

    def xhat_at(k, o, load=None):
        mean, inv, _, _ = norms[k]
        return ((load or load_x[k])(o) - mean) * inv

    def pre_at(k, o):
        load = blocked(x2o) if k == 2 else None
        return xhat_at(k, o, load) * norms[k][2] + norms[k][3]

    def activate(k, store):
        def body(o, _):
            pre = pre_at(k, o)
            store(o, (pre * cdf_of(pre)).astype(BF16))
        chunks(body)

    def slopes(k):
        def body(o, _):
            gps[k][pl.ds(o, CH), :] = slope_of(pre_at(k, o))
        chunks(body)

    moments = sync(0, first, True, begin, prepare_weights)
    small[1].wait()
    small[2].wait()
    norm(0, moments)
    a2a(0, xq, xq, "wait")
    loads[0].wait()
    spans = (Q, 2 * Q)
    for l in range(2):
        act, span = acts[l], spans[l]

        def keep(o, v, act=act):
            act[pl.ds(PAD + o, CH), :] = v

        activate(l, keep)
        for r in range(0, R, 256):
            acc = nn(act[pl.ds(PAD - span + r, 256), :], cw[l, 0])
            acc += nn(act[pl.ds(PAD + r, 256), :], cw[l, 1])
            acc += nn(act[pl.ds(PAD + span + r, 256), :], cw[l, 2])
            if l == 0:
                old = jnp.concatenate([xq[r // Q], xq[r // Q + 1]], axis=0).astype(F32)
            else:
                old = x1[pl.ds(r, 256), :]
            new = old + acc
            if l == 0:
                x1[pl.ds(r, 256), :] = new
            else:
                x2[r // Q] = new[0:Q]
                x2[r // Q + 1] = new[Q:2 * Q]

        def side(l=l, act=act):
            if l == 1:
                a2a(1, x2, x2o, "start")
                x2o[x] = x2[x]
            slopes(l)
            actTs[l][...] = act[pl.ds(PAD, R), :].T

        moments = sync(l + 1, stats(load_x[l + 1]), True, side, (prepare_bias, prepare_counts)[l])
        norm(l + 1, moments)

    full = tracks // TW
    rest = tracks - full * TW
    tiles = full + 1
    half = C // 2
    other = (dp, sq + 1 - 2 * core)

    def rcopy(src, dst, ssem, rsem, dev):
        return pltpu.make_async_remote_copy(
            src_ref=src, dst_ref=dst, send_sem=ssem, recv_sem=rsem, device_id=dev, device_id_type=MESH
        )

    def keep_h(o, v):
        h[o // Q, pl.ds(lax.rem(o, Q), CH), :] = v

    a2a(1, x2, x2o, "wait")
    activate(2, keep_h)
    for k in range(4):
        part = h[k].T
        hT[:, k * Q:(k + 1) * Q] = part
        wide = part.astype(F32)
        for s in range(16):
            sx, sz, sc = s // 4, (s // 2) % 2, s % 2
            to = jnp.where(core == sc, half, 0) + sx * 48 + sz * 24
            dhacc[pl.ds(pl.multiple_of(to, 8), 24), k * Q:(k + 1) * Q] = wide[24 * s:24 * s + 24]
    hPb[0:C] = dhacc[...].astype(BF16)
    ones_row = lax.broadcasted_iota(jnp.int32, (16, R), 0) == 0
    hPb[C:C + 16] = jnp.where(ones_row, 1.0, 0.0).astype(BF16)
    scale = 1.0 / math.sqrt(R * NDEV)

    def piece(rows, counts, bias, at, live):
        v = nn(rows, hT[...])
        for j in range(4):
            z = v[:, j * Q:(j + 1) * Q] + bias
            e = (jnp.exp(z) - counts[:, j * Q:(j + 1) * Q].astype(F32)) * scale
            if live is not None:
                e = jnp.where(lax.broadcasted_iota(jnp.int32, e.shape, 0) < live, e, 0.0)
            dz[at:at + 256, j * Q:(j + 1) * Q] = e.astype(BF16)

    def tile(t, start, tail, turn):
        for i in range(3):
            o = start + i * 256 if tail else pl.multiple_of(start + i * 256, 256)
            if tail and i == 2:
                piece(wtail[...], ttail[...], bcol[pl.ds(o, 256), :], i * 256, rest - 512)
            else:
                piece(wt[pl.ds(o, 256), :], tg[pl.ds(o, 256), :], bcol[pl.ds(o, 256), :], i * 256, None)
        part = nt(hPb[...], dz[...])
        gsend[t] = part[0:half].astype(BF16)
        gown[turn] = part[half:C]
        bb1[0, me1, pl.ds(t, 1), :] = part[C:C + 1]
        add = nn(w[:, pl.ds(start if tail else pl.multiple_of(start, TW), TW)], dz[...])
        dhacc[...] += add
        rcopy(gsend.at[t], grecv.at[t], gcs.at[t], gcr.at[t], other).start()

    def chip(t, slot):
        rcopy(gsend.at[t], grecv.at[t], gcs.at[t], gcr.at[t], other).wait()
        for k in range(4):
            xsend[t, k] = (gown[slot, k * 48:(k + 1) * 48] + grecv[t, k * 48:(k + 1) * 48].astype(F32)).astype(BF16)

    def xstart(t):
        for d in range(1, 4):
            slot, dev = peerx(d)
            rcopy(xsend.at[t, slot], xrecv.at[t, x], gxs.at[t, slot], gxr.at[t, x], dev).start()

    def owner(t, i):
        return t, x * 4 + i * 2 + core

    def yz(t, i):
        return rcopy(ysend.at[t, i], yrecv.at[me2], gys.at[t, i], gyr.at[me2], owner(t, i))

    def spread_rows(t, total):
        for i in range(2):
            ysend[t, i] = total[i * 24:i * 24 + 24].astype(BF16)

            @pl.when(jnp.logical_or(dp != t, zl != i))
            def _(i=i):
                yz(t, i).start()

    def ystart(t):
        total = xsend[t, x].astype(F32)
        for d in range(1, 4):
            slot, dev = peerx(d)
            rcopy(xsend.at[t, slot], xrecv.at[t, slot], gxs.at[t, slot], gxr.at[t, slot], dev).wait()
            total = total + xrecv[t, slot].astype(F32)
        spread_rows(t, total)

    def vstart(t):
        @pl.when(y != t)
        def _():
            rcopy(xsend.at[t], vrecv.at[y], hvs.at[t], hvr.at[y], (zh * 4 + t, sq)).start()

    def vmid():
        for d in range(1, 4):
            slot, dev = peery(d)
            rcopy(vrecv.at[slot], vrecv.at[slot], hvs.at[slot], hvr.at[slot], dev).wait_recv()
        for k in range(4):
            total = xsend[y, k].astype(F32)
            for d in range(1, 4):
                total = total + vrecv[lax.rem(y + d, 4), k].astype(F32)
            vsend[k] = total.astype(BF16)
        for d in range(1, 4):
            slot, dev = peerx(d)
            rcopy(vsend.at[slot], vx.at[x], hxs.at[slot], hxr.at[x], dev).start()

    def vend():
        total = vsend[x].astype(F32)
        for d in range(1, 4):
            slot, dev = peerx(d)
            rcopy(vsend.at[slot], vx.at[slot], hxs.at[slot], hxr.at[slot], dev).wait()
            total = total + vx[slot].astype(F32)
        spread_rows(y, total)
        for d in range(1, 4):
            slot, dev = peery(d)
            rcopy(xsend.at[slot], vrecv.at[slot], hvs.at[slot], hvr.at[slot], dev).wait_send()

    def finish_head():
        @pl.when(dp < tiles)
        def _():
            near = dp < 4

            def body(d, total):
                slot = jnp.where(near, y * 4 + lax.rem(me2 + d, 4), lax.rem(me2 + d, 16))
                rcopy(yrecv.at[slot], yrecv.at[slot], gys.at[0, 0], gyr.at[slot], dev2(slot)).wait_recv()
                return total + yrecv[slot].astype(F32)
            total = lax.fori_loop(1, jnp.where(near, 4, 16), body, ysend[dp, zl].astype(F32))
            fall[dp] = total.astype(BF16)

            @pl.loop(1, 8)
            def _(d):
                slot = lax.rem(dp + d, 8)
                rcopy(fall.at[dp], fall.at[dp], gfs.at[slot], gfr.at[dp], (slot, sq)).start()

    def collect_head():
        @pl.loop(0, tiles)
        def _(t):
          @pl.when(jnp.logical_or(t >= 4, t == y))
          def _():
            for i in range(2):
                @pl.when(jnp.logical_or(dp != t, zl != i))
                def _(i=i):
                    yz(t, i).wait_send()

        @pl.when(dp < tiles)
        def _():
            @pl.loop(1, 8)
            def _(d):
                slot = lax.rem(dp + d, 8)
                rcopy(fall.at[dp], fall.at[dp], gfs.at[slot], gfr.at[dp], (slot, sq)).wait_send()

        for t in range(tiles):
            @pl.when(dp != t)
            def _(t=t):
                rcopy(fall.at[t], fall.at[t], gfs.at[0], gfr.at[t], (t, sq)).wait_recv()
        for t in range(full):
            ghead_ref[:, t * TW:(t + 1) * TW] = fall[t].astype(F32)
        ghead_ref[:, full * TW:tracks] = fall[full].astype(F32)[:, 0:rest]
        pltpu.make_async_copy(ghead_ref, ghead_hbm, out_sem.at[1]).start()

    def bias_start():
        exchange(bb1, 0, me1, 8, peer1, e1_sem, q1_sem, "start")

    def bias_row(t):
        return rcopy(brow.at[t], bin_.at[me2], brs.at[t], brr.at[me2], dev2(t))

    def bias_middle():
        exchange(bb1, 0, me1, 8, peer1, e1_sem, q1_sem, "wait")
        total = functools.reduce(lambda a, b: a + b, [bb1[0, i] for i in range(8)])
        for t in range(tiles):
            brow[t] = total[t:t + 1]

            @pl.when(me2 != t)
            def _(t=t):
                bias_row(t).start()

    def bias_own():
        @pl.when(me2 < tiles)
        def _():
            def body(d, total):
                slot, dev = peer2(d)
                rcopy(bin_.at[slot], bin_.at[slot], brs.at[0], brr.at[slot], dev).wait_recv()
                return total + bin_[slot]
            ball[me2] = lax.fori_loop(1, 16, body, brow[me2])

            @pl.loop(1, 16)
            def _(d):
                slot, dev = peer2(d)
                rcopy(ball.at[me2], ball.at[me2], e2_sem.at[slot], q2_sem.at[me2], dev).start()

    def bias_end():
        for t in range(tiles):
            n = min(TW, tracks - t * TW)

            @pl.when(me2 != t)
            def _(t=t):
                bias_row(t).wait_send()
                rcopy(ball.at[t], ball.at[t], e2_sem.at[0], q2_sem.at[t], dev2(t)).wait_recv()
            gbias_ref[pl.ds(t * TW, n)] = ball[t][0, 0:n]

        @pl.when(me2 < tiles)
        def _():
            @pl.loop(1, 16)
            def _(d):
                slot, dev = peer2(d)
                rcopy(ball.at[me2], ball.at[me2], e2_sem.at[slot], q2_sem.at[me2], dev).wait_send()

    dhacc[...] = jnp.zeros(dhacc.shape, F32)

    def near(i):
        return lax.rem(y + 1 + i, 4)

    @pl.loop(0, 3)
    def _(i):
        tile(near(i), near(i) * TW, False, i % 2)

        @pl.when(i > 0)
        def _():
            chip(near(i - 1), (i + 1) % 2)
            vstart(near(i - 1))

    tile(full, full * TW, True, 1)
    chip(near(2), 0)
    vstart(near(2))

    @pl.loop(0, 3)
    def _(i):
        t = jnp.where(i == 0, 4, jnp.where(i == 1, y, 5))
        tile(t, t * TW, False, i % 2)
        chip(jnp.where(i == 0, full, jnp.where(i == 1, 4, y)), (i + 1) % 2)

        @pl.when(i == 0)
        def _():
            xstart(full)

    class Job:
        def __init__(self, number, layer, taps, at, ring, me, peer, dev):
            self.q, self.layer, self.taps, self.at, self.ring = number, layer, taps, at, ring
            self.me, self.peer, self.dev, self.owners = me, peer, dev, 3 * len(taps)

    jobs = (
        Job(0, 1, (0, 1, 2), y, peery, me3, peer3, dev3),
        Job(1, 0, (0, 2), x, peerx, me2, peer2, dev2),
        Job(2, 0, (1,), y, peery, me3, peer3, dev3),
    )

    def conv_start(l, span, actT, taps):
        for j in taps:
            cfull[j] = nn(actT[...], gpad[pl.ds(PAD + (1 - j) * span, R), :])
            csend[l, j] = cfull[j, pl.ds(pl.multiple_of((1 - core) * half, 64), half), :].astype(BF16)
            rcopy(csend.at[l, j], crecv.at[l, j], ccs.at[l, j], ccr.at[l, j], other).start()

    def conv_x(job):
        l, q = job.layer, job.q
        for i, j in enumerate(job.taps):
            rcopy(csend.at[l, j], crecv.at[l, j], ccs.at[l, j], ccr.at[l, j], other).wait()
            for k in range(4):
                mine = cfull[j, pl.ds(pl.multiple_of(core * half + k * 48, 16), 48), :]
                cx[q, i, k] = (mine + crecv[l, j, k * 48:(k + 1) * 48].astype(F32)).astype(BF16)
            for d in range(1, 4):
                slot, dev = job.ring(d)
                rcopy(cx.at[q, i, slot], cxr.at[q, i, job.at], cxs.at[q, i, slot], cxrs.at[q, i, job.at], dev).start()

    def block(job, i):
        q, me = job.q, job.me
        return rcopy(cy.at[q, i], cyr.at[q, me], cys.at[q, i], cyrs.at[q, me], job.dev(i))

    def conv_rs(job):
        q = job.q
        for j in range(len(job.taps)):
            total = cx[q, j, job.at].astype(F32)
            for d in range(1, 4):
                slot, dev = job.ring(d)
                rcopy(cx.at[q, j, slot], cxr.at[q, j, slot], cxs.at[q, j, slot], cxrs.at[q, j, slot], dev).wait()
                total = total + cxr[q, j, slot].astype(F32)
            for b in range(3):
                i = 3 * j + b
                cy[q, i] = total[b * 16:(b + 1) * 16].astype(BF16)

                @pl.when(job.me != i)
                def _(i=i):
                    block(job, i).start()

    def piece_of(job):
        return cz.at[job.q, job.me // 3, job.me % 3]

    def conv_ag(job):
        q = job.q

        @pl.when(job.me < job.owners)
        def _():
            def body(d, total):
                slot, dev = job.peer(d)
                rcopy(cyr.at[q, slot], cyr.at[q, slot], cys.at[q, 0], cyrs.at[q, slot], dev).wait_recv()
                return total + cyr[q, slot].astype(F32)
            total = lax.fori_loop(1, 16, body, cy[q, job.me].astype(F32))
            cz[q, job.me // 3, job.me % 3] = total.astype(BF16)

            @pl.loop(1, 16)
            def _(d):
                slot, dev = job.peer(d)
                rcopy(piece_of(job), piece_of(job), czs.at[q, slot], czrs.at[q, job.me], dev).start()

    def conv_xag(job):
        q = job.q
        for j in range(len(job.taps)):
            for b in range(3):
                i = 3 * j + b

                @pl.when(job.me != i)
                def _(i=i, j=j, b=b):
                    rcopy(cz.at[q, j, b], cz.at[q, j, b], czs.at[q, 0], czrs.at[q, i], job.dev(i)).wait_recv()
            for d in range(1, 4):
                slot, dev = job.ring(d)
                rcopy(cz.at[q, j], ca.at[q, j, job.at], cas.at[q, j, slot], cars.at[q, j, job.at], dev).start()
            ca[q, j, job.at] = cz[q, j]

    def put(job, i, side):
        src = (ca, cb)[side].at[job.q, i]
        at = 1 - core if side else core
        return pltpu.make_async_copy(src, gconv_hbm.at[job.layer, job.taps[i], at], oc_sem.at[job.q, i, side])

    def conv_cag(job):
        q = job.q
        for i, j in enumerate(job.taps):
            for d in range(1, 4):
                slot, dev = job.ring(d)
                rcopy(cz.at[q, i], ca.at[q, i, slot], cas.at[q, i, slot], cars.at[q, i, slot], dev).wait()
            rcopy(ca.at[q, i], cb.at[q, i], cbs.at[q, i], cbrs.at[q, i], other).start()
            put(job, i, 0).start()

    def conv_end(job):
        q = job.q
        for i, j in enumerate(job.taps):
            rcopy(ca.at[q, i], cb.at[q, i], cbs.at[q, i], cbrs.at[q, i], other).wait()
            put(job, i, 1).start()
        for i in range(job.owners):
            @pl.when(job.me != i)
            def _(i=i):
                block(job, i).wait_send()

        @pl.when(job.me < job.owners)
        def _():
            @pl.loop(1, 16)
            def _(d):
                slot, dev = job.peer(d)
                rcopy(piece_of(job), piece_of(job), czs.at[q, slot], czrs.at[q, job.me], dev).wait_send()

    n = float(R * NDEV)

    def sums(k, load):
        def body(o, acc):
            v = load(o) * gps[k][pl.ds(o, CH), :]
            dpre[pl.ds(o, CH), :] = v
            return acc[0] + fold(v), acc[1] + fold(v * xhat_at(k, o))
        zero = jnp.zeros((8, C), F32)
        a, b = chunks(body, (zero, zero))
        return jnp.concatenate([jnp.sum(a, axis=0, keepdims=True), jnp.sum(b, axis=0, keepdims=True)], axis=0)

    def report(k, s):
        gshift_ref[k:k + 1, :] = s[0:1]
        ggain_ref[k:k + 1, :] = s[1:2]

    def dv_at(k, o, s):
        _, inv, gain, _ = norms[k]
        v = blocked(dpq)(o) if k == 2 else dpre[pl.ds(o, CH), :]
        return gain * inv * (v - s[0:1] * (1.0 / n) - xhat_at(k, o) * (s[1:2] * (1.0 / n)))

    def back(o, acc):
        k = o // Q
        v = dpre[pl.ds(o, CH), :] * slope_of(pre_at(2, o))
        dps[k, pl.ds(lax.rem(o, Q), CH), :] = v.astype(BF16)
        return acc[0] + fold(v), acc[1] + fold(v * xhat_at(2, o, blocked(x2o)))

    for k in range(4):
        dpre[k * Q:(k + 1) * Q] = dhacc[:, k * Q:(k + 1) * Q].T
    zero = jnp.zeros((8, C), F32)
    left, right = chunks(back, (zero, zero))
    value = jnp.concatenate([jnp.sum(left, axis=0, keepdims=True), jnp.sum(right, axis=0, keepdims=True)], axis=0)

    def fill31():
        bias_start()
        a2a(2, dps, dpq, "start")
        dpq[x] = dps[x]
        xstart(4)
        chip(5, 0)
        xstart(5)

    def fill32():
        bias_middle()
        ystart(full)

    s = sync(3, value, False, fill31, fill32)
    report(2, s)
    a2a(2, dps, dpq, "wait")

    for l in (1, 0):
        span = spans[l]

        def spread(o, _, l=l, s=s):
            v = dv_at(l + 1, o, s)
            if l == 0:
                v = v + g[pl.ds(o, CH), :]
            g[pl.ds(o, CH), :] = v
            gpad[pl.ds(PAD + o, CH), :] = v.astype(BF16)

        chunks(spread)
        if l == 0:
            conv_start(0, span, actTs[0], (0, 1, 2))
        for r in range(0, R, 256):
            acc = nt(gpad[pl.ds(PAD + span + r, 256), :], cw[l, 0])
            acc += nt(gpad[pl.ds(PAD + r, 256), :], cw[l, 1])
            acc += nt(gpad[pl.ds(PAD - span + r, 256), :], cw[l, 2])
            dpre[pl.ds(r, 256), :] = acc

        if l == 0:
            conv_x(jobs[1])
            conv_x(jobs[2])
        value = sums(l, lambda o: dpre[pl.ds(o, CH), :])

        def early(l=l, span=span):
            if l == 0:
                conv_rs(jobs[0])
                _, inv, gain, _ = norms[0]

                def body(o, _):
                    v = g[pl.ds(o, CH), :] + gain * inv * dpre[pl.ds(o, CH), :]
                    asend[o // Q, pl.ds(lax.rem(o, Q), CH), :] = v.astype(BF16)
                chunks(body)
                conv_rs(jobs[2])
                conv_rs(jobs[1])
                a2a(3, asend, arecv, "start")
                arecv[x] = asend[x]
            else:
                conv_start(1, span, actTs[1], (0, 1, 2))
                vmid()

        def late(l=l):
            if l == 1:
                conv_x(jobs[0])
                ystart(4)
                ystart(5)
                vend()
                bias_own()
            else:
                conv_ag(jobs[2])
                conv_ag(jobs[1])
                conv_ag(jobs[0])
                finish_head()

        s = sync(5 - l, value, False, early, late)
        report(l, s)

    a2a(3, asend, arecv, "wait")
    mean, inv, gain, _ = norms[0]

    def finish(o, _):
        xh = (seq_ref[pl.ds(o, CH), :].astype(F32) - mean) * inv
        part = blocked(arecv)(o)
        g[pl.ds(o, CH), :] = part - gain * inv * (s[0:1] * (1.0 / n) + xh * (s[1:2] * (1.0 / n)))
    chunks(finish)
    put_in = pltpu.make_async_copy(g, gin_hbm, out_sem.at[0])
    put_in.start()
    conv_xag(jobs[2])
    conv_xag(jobs[1])
    conv_xag(jobs[0])
    bias_end()
    collect_head()
    conv_cag(jobs[2])
    conv_cag(jobs[1])
    conv_cag(jobs[0])
    conv_end(jobs[2])
    conv_end(jobs[1])
    conv_end(jobs[0])
    put_in.wait()
    pltpu.make_async_copy(ghead_ref, ghead_hbm, out_sem.at[1]).wait()
    for job in jobs:
        for i in range(len(job.taps)):
            put(job, i, 0).wait()
            put(job, i, 1).wait()


def emit(gin, ggain, gshift, ghead, gbias, gconv, *rest):
    outs, bufs, wide, isem, osem = rest[:6], rest[6:12], rest[12], rest[13], rest[14]
    ins = [pltpu.make_async_copy(src, dst, isem.at[i]) for i, (src, dst) in
           enumerate(zip((gin, ggain, gshift, ghead, gbias), bufs))]
    taps = [pltpu.make_async_copy(gconv.at[j], bufs[5].at[j], isem.at[5 + j]) for j in range(6)]
    for cp in taps + ins:
        cp.start()
    back = [pltpu.make_async_copy(src, dst, osem.at[i]) for i, (src, dst) in
            enumerate(zip(bufs, (outs[0], outs[2], outs[3], outs[4], outs[5])))]
    send = [pltpu.make_async_copy(wide.at[j], outs[1].at[j], osem.at[5 + j]) for j in range(6)]
    for j in range(6):
        taps[j].wait()
        wide[j] = bufs[5][j].astype(F32)
        send[j].start()
    for a, b in zip(ins, back):
        a.wait()
        b.start()
    for cp in send + back:
        cp.wait()


def on_device(sequence, conv_weight, gains, shifts, head_weight, head_bias, targets):
    tracks = head_weight.shape[1]
    vmem = pl.BlockSpec(memory_space=pltpu.VMEM)
    hbm = pl.BlockSpec(memory_space=pl.ANY)
    sds = jax.ShapeDtypeStruct
    V = pltpu.VMEM
    D = pltpu.SemaphoreType.DMA
    T7 = tracks // TW + 1
    W7 = T7 * TW
    gin, ggain, gshift, ghead, gbias, gconv = pl.pallas_call(
        kernel,
        out_shape=(
            sds((R, C), F32), sds((3, C), F32), sds((3, C), F32), sds((C // 16, tracks), F32), sds((tracks,), F32),
            sds((2, 3, 2, 4, 3, 16, C), BF16),
        ),
        in_specs=[hbm] * 7,
        out_specs=(hbm, vmem, vmem, hbm, vmem, hbm),
        scratch_shapes=[
            V((R, C), BF16), V((3, C), F32), V((3, C), F32), V((tracks,), F32), V((C // 16, tracks), F32),
            V((2, 3, C, C), BF16), V((tracks, C), BF16), V((256, C), BF16), V((C, W7), BF16),
            V((tracks, R), jnp.int32), V((256, R), jnp.int32), V((W7, Q), F32), V((48, Q), F32),
            V((4, Q, C), BF16), V((R, C), F32), V((4, Q, C), F32), V((4, Q, C), F32),
            V((R + 2 * PAD, C), BF16), V((R + 2 * PAD, C), BF16), V((C, R), BF16), V((C, R), BF16),
            V((C, R), BF16), V((C + 16, R), BF16), V((TW, R), BF16),
            V((C, R), F32), V((4, Q, C), BF16), V((4, Q, C), BF16),
            V((R, C), F32), V((R, C), F32), V((R + 2 * PAD, C), BF16), V((R, C), F32), V((R, C), F32),
            V((4, Q, C), BF16),
            V((6, 8, 2, C), F32), V((6, 16, 2, C), F32), V((1, 8, 8, TW), F32), V((8, 1, TW), F32), V((16, 1, TW), F32), V((8, 1, TW), F32),
            V((T7, 192, TW), BF16), V((T7, 192, TW), BF16), V((2, 192, TW), F32),
            V((T7, 4, 48, TW), BF16), V((T7, 4, 48, TW), BF16), V((T7, 2, 24, TW), BF16), V((16, 24, TW), BF16), V((T7, 24, TW), BF16),
            V((4, 4, 48, TW), BF16), V((4, 48, TW), BF16), V((4, 48, TW), BF16),
            V((3, C, C), F32), V((2, 3, C // 2, C), BF16), V((2, 3, C // 2, C), BF16), V((3, 3, 4, 48, C), BF16),
            V((3, 3, 4, 48, C), BF16), V((3, 9, 16, C), BF16), V((3, 16, 16, C), BF16), V((3, 3, 3, 16, C), BF16),
            V((3, 3, 4, 3, 16, C), BF16), V((3, 3, 4, 3, 16, C), BF16),
            D((10,)), D((8,)), D((16,)), D((6, 8)), D((6, 16)), D((4, 4)), D((4, 4)),
            D((8,)), D((16,)), D((1, 8)), D((8,)), D((8,)), D((16,)), D((T7,)), D((T7,)), D((T7, 4)), D((T7, 4)), D((T7, 2)), D((16,)),
            D((8,)), D((T7,)), D((4,)), D((4,)), D((4,)), D((4,)),
            D((2,)), D((3, 3, 2)), D((2, 3)), D((2, 3)), D((3, 3, 4)), D((3, 3, 4)), D((3, 9)), D((3, 16)), D((3, 16)), D((3, 9)), D((3, 3, 4)), D((3, 3, 4)),
            D((3, 3)), D((3, 3)),
        ],
        compiler_params=pltpu.CompilerParams(
            collective_id=0, has_side_effects=True, vmem_limit_bytes=67043328
        ),
        name="whole",
    )(sequence.reshape(R, C), gains, shifts, head_bias, conv_weight, head_weight.T, jnp.transpose(targets, (2, 0, 1)))
    gin, grad_conv, ggain, gshift, ghead, gbias = pl.pallas_call(
        emit,
        out_shape=(
            sds((R, C), F32), sds((6, C, C), F32), sds((3, C), F32), sds((3, C), F32), sds((C // 16, tracks), F32),
            sds((tracks,), F32),
        ),
        in_specs=[hbm] * 6,
        out_specs=(hbm,) * 6,
        scratch_shapes=[
            V((R, C), F32), V((3, C), F32), V((3, C), F32), V((C // 16, tracks), F32), V((tracks,), F32),
            V((6, C, C), BF16), V((6, C, C), F32), D((11,)), D((11,)),
        ],
        name="emit",
    )(gin, ggain, gshift, ghead, gbias, gconv.reshape(6, C, C))
    return gin.reshape(1, R, C), grad_conv.reshape(2, 3, C, C), ggain, gshift, ghead, gbias


def solution(mesh):
    rep = P()
    return jax.shard_map(
        on_device,
        mesh=mesh,
        in_specs=(P("dp", "seq", None), rep, rep, rep, rep, rep, P("dp", "seq", None)),
        out_specs=(P("dp", "seq", None), rep, rep, rep, P("seq", None), rep),
        check_vma=False,
    )
```
